32 devices in a mesh: rep: 8 (over z, y), fsdp: 4 (over x, core).
Axes of the slice: x: 2, y: 2, z: 4, core: 2. Of those that a mesh axis runs over, the one named last changes fastest.
Arguments:
- tokens: bfloat16 [16384, 768], P(('rep', 'fsdp')), may hold values from -6 to 6
- prefix: int32 [64], P(('rep', 'fsdp')), may hold values from 25 to 128
- cotangent: bfloat16 [16384, 768], P(('rep', 'fsdp')), may hold values from -6 to 6
- w_query: bfloat16 [768, 768], P('fsdp'), may hold values from -0.21875 to 0.21875
- b_query: bfloat16 [768], P('fsdp'), may hold values from -3 to 3
- w_key: bfloat16 [768, 768], P('fsdp'), may hold values from -0.21875 to 0.21875
- w_value: bfloat16 [768, 768], P('fsdp'), may hold values from -0.21875 to 0.21875
- b_value: bfloat16 [768], P('fsdp'), may hold values from -3 to 3
- w_out: bfloat16 [768, 768], P('fsdp'), may hold values from -1.25 to 1.25
- b_out: bfloat16 [768], P('fsdp'), may hold values from -3 to 3
- gain_one: bfloat16 [768], P('fsdp'), may hold values from 0.25 to 1.75
- shift_one: bfloat16 [768], P('fsdp'), may hold values from -2 to 2
- w_up: bfloat16 [768, 3072], P('fsdp'), may hold values from -0.21875 to 0.21875
- b_up: bfloat16 [3072], P('fsdp'), may hold values from -3 to 3
- w_down: bfloat16 [3072, 768], P('fsdp'), may hold values from -0.109375 to 0.109375
- b_down: bfloat16 [768], P('fsdp'), may hold values from -2 to 2
- gain_two: bfloat16 [768], P('fsdp'), may hold values from 0.25 to 1.75
- shift_two: bfloat16 [768], P('fsdp'), may hold values from -2 to 2
Outputs:
- layer_out: bfloat16 [16384, 768], P(('rep', 'fsdp'))
- token_grad: float32 [16384, 768], P(('rep', 'fsdp'))
- grad_w_query: float32 [768, 768], P('fsdp')
- grad_b_query: float32 [768], P('fsdp')
- grad_w_key: float32 [768, 768], P('fsdp')
- grad_w_value: float32 [768, 768], P('fsdp')
- grad_b_value: float32 [768], P('fsdp')
- grad_w_out: float32 [768, 768], P('fsdp')
- grad_b_out: float32 [768], P('fsdp')
- grad_gain_one: float32 [768], P('fsdp')
- grad_shift_one: float32 [768], P('fsdp')
- grad_w_up: float32 [768, 3072], P('fsdp')
- grad_b_up: float32 [3072], P('fsdp')
- grad_w_down: float32 [3072, 768], P('fsdp')
- grad_b_down: float32 [768], P('fsdp')
- grad_gain_two: float32 [768], P('fsdp')
- grad_shift_two: float32 [768], P('fsdp')
The draws below stay inside these ranges and needn't reach their ends.
All inputs are finite; a program needn't handle non-finite values.
Results may differ from the reference program's by a relative error of at most 0.024.
Values may be sent and summed in bfloat16 or wider, within the bound.
A program may use at most 128 MiB of HBM per device.

```python
import math
import jax
import jax.numpy as jnp
from jax import lax

D = 768
H = 12
HD = 64
FF = 3072
LEN = 256
SEQS = 64
TOKENS = 16384


def place_ends(array, key, smallest, top_value):
    index_at = [jax.random.randint(jax.random.fold_in(key, axis), (), 0, length) for axis, length in enumerate(array.shape)]
    longest = array.shape.index(max(array.shape))
    neighbour = index_at[:longest] + [(index_at[longest] + 1) % array.shape[longest]] + index_at[longest + 1:]
    return array.at[tuple(index_at)].set(smallest).at[tuple(neighbour)].set(top_value)


def raised(array, stream_key, source, target, blocks, factor):
    owner, partner = [(jnp.arange(array.shape[position]) // (array.shape[position] // blocks)).reshape([-1 if axis == position else 1 for axis in range(array.ndim)]) for position in (source, target)]
    chosen = jax.random.permutation(stream_key, blocks)[partner]
    strong = (owner == chosen) | (owner == (partner + blocks // 2) % blocks)
    return jnp.where(strong, factor * array, array)


def block_levels(own_key, dims, shards, smallest, top_value):
    factor_of, own = 1.0, jax.random.fold_in(own_key, 6)
    for axis_at, blocks in shards:
        steps = jnp.exp(jax.random.uniform(jax.random.fold_in(own, axis_at), (blocks,), jnp.float32, smallest / len(shards), top_value / len(shards)))
        factor_of = factor_of * jnp.repeat(steps, dims[axis_at] // blocks).reshape([-1 if axis == axis_at else 1 for axis in range(len(dims))])
    return factor_of


def bell_draw(own_key, extent, spread, limit, split=(), held_as=jnp.bfloat16):
    loudness = block_levels(own_key, extent, split, -0.22, 0.18) if split else 1.0
    array = jax.random.normal(own_key, extent, jnp.float32) * spread * loudness
    return jnp.minimum(jnp.maximum(array, -limit), limit).astype(held_as)


def heavy_noise(key, dims, spread, bound, cuts, heavy, kind=jnp.bfloat16):
    drawn = spread * jax.random.normal(key, dims, jnp.float32)
    if cuts:
        drawn = drawn * block_levels(key, dims, cuts, -0.22, 0.18)
    return jnp.clip(raised(drawn, jax.random.fold_in(key, 3), *heavy), -bound, bound).astype(kind)


def setup_inputs(seed: int = 0) -> dict:
    streams_of = jax.random.split(jax.random.key(seed), 19)
    return {
        "tokens": bell_draw(streams_of[0], (TOKENS, D), 1.0, 6.0, ((0, 32),)),
        "prefix": place_ends(jax.random.randint(streams_of[1], (SEQS,), LEN // 10, LEN // 2 + 1), jax.random.fold_in(streams_of[1], 1), LEN // 10, (LEN // 2 + 1) - 1).astype(jnp.int32),
        "cotangent": heavy_noise(streams_of[2], (TOKENS, D), 1.0, 6.0, ((0, 32),), (0, 1, 32, 2.75)),
        "w_query": bell_draw(streams_of[3], (D, D), D ** -0.5, 0.21875, ((0, 4),)),
        "b_query": bell_draw(streams_of[4], (D,), 0.5, 3.0, ((0, 4),)),
        "w_key": bell_draw(streams_of[5], (D, D), D ** -0.5, 0.21875, ((0, 4),)),
        "w_value": bell_draw(streams_of[6], (D, D), D ** -0.5, 0.21875, ((0, 4),)),
        "b_value": bell_draw(streams_of[7], (D,), 0.5, 3.0, ((0, 4),)),
        "w_out": bell_draw(streams_of[8], (D, D), (max(D * 8 // LEN, 1)) ** -0.5, 1.25, ((0, 4),)),
        "b_out": bell_draw(streams_of[9], (D,), 0.5, 3.0, ((0, 4),)),
        "gain_one": jnp.clip(1.0 + 0.15 * jax.random.normal(streams_of[10], (D,), jnp.float32), 0.25, 1.75).astype(jnp.bfloat16),
        "shift_one": bell_draw(streams_of[11], (D,), 0.3, 2.0, ((0, 4),)),
        "w_up": bell_draw(streams_of[12], (D, FF), D ** -0.5, 0.21875, ((0, 4),)),
        "b_up": bell_draw(streams_of[13], (FF,), 0.5, 3.0, ((0, 4),)),
        "w_down": bell_draw(streams_of[14], (FF, D), FF ** -0.5, 0.109375, ((0, 4),)),
        "b_down": bell_draw(streams_of[15], (D,), 0.3, 2.0, ((0, 4),)),
        "gain_two": jnp.clip(1.0 + 0.15 * jax.random.normal(streams_of[16], (D,), jnp.float32), 0.25, 1.75).astype(jnp.bfloat16),
        "shift_two": bell_draw(streams_of[17], (D,), 0.3, 2.0, ((0, 4),)),
    }


@jax.custom_vjp
def low(v):
    return lax.optimization_barrier(v.astype(jnp.bfloat16)).astype(jnp.float32)

@jax.custom_vjp
def low_back(v):
    return v

def low_keep(v):
    return (low(v), None)

def low_pass(kept, grad):
    return (grad,)

def back_keep(v):
    return (v, None)

def back_low(kept, grad):
    return (low(grad),)
low.defvjp(low_keep, low_pass)
low_back.defvjp(back_keep, back_low)
epsilon = 1e-12
precise = lax.Precision.HIGHEST

def round_both(value):
    return low(low_back(value))

def norm_rows(hidden, gain_vec, shift_vec):
    centre = hidden - lax.optimization_barrier(jnp.mean(hidden, axis=-1, keepdims=True))
    spread_sq = lax.optimization_barrier(jnp.mean(centre * centre, axis=-1, keepdims=True))
    return centre * lax.rsqrt(spread_sq + epsilon) * gain_vec + shift_vec

def attention(query_rows, key_rows, value_rows, prefix_limit):
    query_heads = query_rows.reshape(LEN, H, HD)
    key_heads = key_rows.reshape(LEN, H, HD)
    value_heads = value_rows.reshape(LEN, H, HD)
    scores = jnp.einsum('qhd,khd->hqk', query_heads, key_heads, precision=precise) * HD ** (-0.5)
    scores = low_back(scores)
    row_pos = jnp.arange(LEN)[:, None]
    col_pos = jnp.arange(LEN)[None, :]
    visible = (col_pos <= row_pos) | (col_pos < prefix_limit)
    scores = jnp.where(visible[None], scores, -1e+30)
    prob = round_both(jax.nn.softmax(scores, axis=-1))
    context = jnp.einsum('hqk,khd->qhd', prob, value_heads, precision=precise)
    return context.reshape(LEN, D)

def block_forward(group_rows, group_prefix, params):
    w_query, b_query, w_key, w_value, b_value, w_out, b_out, gain_one, shift_one, w_up, b_up, w_down, b_down, gain_two, shift_two = params
    group_size = group_rows.shape[0]
    flat_rows = group_rows.reshape(-1, D)
    query_rows = round_both(jnp.dot(flat_rows, w_query, precision=precise) + b_query)
    key_rows = round_both(jnp.dot(flat_rows, w_key, precision=precise))
    value_rows = round_both(jnp.dot(flat_rows, w_value, precision=precise) + b_value)
    context = jax.vmap(attention)(query_rows.reshape(group_size, LEN, D), key_rows.reshape(group_size, LEN, D), value_rows.reshape(group_size, LEN, D), group_prefix)
    context = round_both(context.reshape(-1, D))
    attn_out = low_back(jnp.dot(context, w_out, precision=precise) + b_out)
    inner_rows = low(norm_rows(flat_rows + attn_out, gain_one, shift_one))
    upward = low_back(jnp.dot(inner_rows, w_up, precision=precise) + b_up)
    active = low(jax.nn.gelu(upward, approximate=False))
    downward = low_back(jnp.dot(active, w_down, precision=precise) + b_down)
    return norm_rows(inner_rows + downward, gain_two, shift_two)

def reference(tokens, prefix, cotangent, w_query, b_query, w_key, w_value, b_value, w_out, b_out, gain_one, shift_one, w_up, b_up, w_down, b_down, gain_two, shift_two):
    params = tuple((item.astype(jnp.float32) for item in (w_query, b_query, w_key, w_value, b_value, w_out, b_out, gain_one, shift_one, w_up, b_up, w_down, b_down, gain_two, shift_two)))
    group_size = math.gcd(SEQS, max(1, 4096 // LEN))
    steps_count = SEQS // group_size
    all_rows = tokens.astype(jnp.float32).reshape(steps_count, group_size, LEN, D)
    all_grads = cotangent.astype(jnp.float32).reshape(steps_count, group_size * LEN, D)
    all_prefix = prefix.reshape(steps_count, group_size)

    def group_step(grad_sum, batch_item):
        group_rows, group_prefix, group_cot = batch_item
        out_rows, pullback = jax.vjp(lambda rows_in, params_in: block_forward(rows_in, group_prefix, params_in), group_rows, params)
        row_grad, param_grad = pullback(group_cot)
        grad_sum = jax.tree.map(jnp.add, grad_sum, param_grad)
        return (grad_sum, (out_rows.astype(jnp.bfloat16), row_grad))
    zero_grads = tuple((jnp.zeros_like(item) for item in params))
    grad_sum, (out_all, grad_all) = lax.scan(group_step, zero_grads, (all_rows, all_prefix, all_grads))
    layer_out = out_all.reshape(TOKENS, D)
    token_grad = grad_all.reshape(TOKENS, D)
    return (layer_out, token_grad, grad_sum[0], grad_sum[1], grad_sum[2], grad_sum[3], grad_sum[4], grad_sum[5], grad_sum[6], grad_sum[7], grad_sum[8], grad_sum[9], grad_sum[10], grad_sum[11], grad_sum[12], grad_sum[13], grad_sum[14])
```

```python
import functools

import jax
import jax.numpy as jnp
from jax import lax
from jax.experimental import pallas as pl
from jax.experimental.pallas import tpu as pltpu
from jax.sharding import PartitionSpec as P

H = 12
HD = 64
PAIR = 2 * HD

epsilon = 1e-12
masked_fill = -1e30


def as_float(vector):
    return vector.astype(jnp.float32)


def product(left, right):
    return jnp.dot(left, right, preferred_element_type=jnp.float32)


def nt(left, right):
    return lax.dot_general(left, right, (((1,), (1,)), ((), ())), preferred_element_type=jnp.float32)


def tn(left, right):
    return lax.dot_general(left, right, (((0,), (0,)), ((), ())), preferred_element_type=jnp.float32)


def normalize(hidden):
    centre = hidden - jnp.mean(hidden, axis=-1, keepdims=True)
    inverse = lax.rsqrt(jnp.mean(centre * centre, axis=-1, keepdims=True) + epsilon)
    return (centre * inverse, inverse)


def norm_back(grad_norm, normed, inverse):
    mean_grad = jnp.mean(grad_norm, axis=-1, keepdims=True)
    mean_cross = jnp.mean(grad_norm * normed, axis=-1, keepdims=True)
    return inverse * (grad_norm - mean_grad - normed * mean_cross)


def softmax_parts(query, key, limit):
    length = query.shape[0]
    scores = nt(query, key) * HD ** (-0.5)
    row_pos = lax.broadcasted_iota(jnp.int32, (length, length), 0)
    col_pos = lax.broadcasted_iota(jnp.int32, (length, length), 1)
    visible = (col_pos <= row_pos) | (col_pos < limit)
    scores = jnp.where(visible, scores, masked_fill)
    expo = jnp.exp(scores - jnp.max(scores, axis=-1, keepdims=True))
    return expo * (1.0 / jnp.sum(expo, axis=-1, keepdims=True))


def attend_kernel(prefix_ref, q_ref, k_ref, v_ref, out_ref):
    limit = prefix_ref[pl.program_id(0)]
    outs = []
    for head in range(2):
        cols = slice(head * HD, (head + 1) * HD)
        prob = softmax_parts(q_ref[:, cols], k_ref[:, cols], limit)
        outs.append(product(prob.astype(jnp.bfloat16), v_ref[:, cols]))
    out_ref[...] = jnp.concatenate(outs, axis=1).astype(jnp.bfloat16)


def attend_back_kernel(prefix_ref, q_ref, k_ref, v_ref, d_ref, dq_ref, dk_ref, dv_ref):
    limit = prefix_ref[pl.program_id(0)]
    d_q, d_k, d_v = [], [], []
    for head in range(2):
        cols = slice(head * HD, (head + 1) * HD)
        query, key, value, d_context = q_ref[:, cols], k_ref[:, cols], v_ref[:, cols], d_ref[:, cols]
        prob = softmax_parts(query, key, limit)
        d_v.append(tn(prob.astype(jnp.bfloat16), d_context))
        d_prob = as_float(nt(d_context, value).astype(jnp.bfloat16))
        weighted = prob * d_prob
        d_scores = (weighted - prob * jnp.sum(weighted, axis=-1, keepdims=True)).astype(jnp.bfloat16)
        d_q.append(product(d_scores, key) * HD ** (-0.5))
        d_k.append(tn(d_scores, query) * HD ** (-0.5))
    for ref, pieces in ((dq_ref, d_q), (dk_ref, d_k), (dv_ref, d_v)):
        ref[...] = jnp.concatenate(pieces, axis=1).astype(jnp.bfloat16)


def attention_call(kernel, prefix, operands, outputs):
    rows, width = operands[0].shape
    length = rows // prefix.shape[0]
    block = pl.BlockSpec((length, PAIR), lambda s, h, p: (s, h))
    shape = jax.ShapeDtypeStruct((rows, width), jnp.bfloat16)
    single = outputs == 1
    return pl.pallas_call(
        kernel,
        out_shape=shape if single else [shape] * outputs,
        grid_spec=pltpu.PrefetchScalarGridSpec(
            num_scalar_prefetch=1,
            grid=(prefix.shape[0], width // PAIR),
            in_specs=[block] * len(operands),
            out_specs=block if single else [block] * outputs,
        ),
        cost_estimate=pl.CostEstimate(
            flops=4 * len(operands) * rows * length * width,
            bytes_accessed=2 * rows * width * (len(operands) + outputs),
            transcendentals=rows * length * H,
        ),
    )(prefix, *operands)


def swap(value, axis, bit):
    size = lax.axis_size(axis)
    return lax.ppermute(value, axis, [(i, i ^ bit) for i in range(size)])


def bits_of(axis):
    size = lax.axis_size(axis)
    assert size & (size - 1) == 0
    return [1 << b for b in range(size.bit_length() - 1)]


def gather(block):
    index = lax.axis_index("fsdp")
    rows = block.shape[0]
    rest = block.shape[1:]
    held = block.reshape((1, rows) + rest)
    done = 1
    for bit in reversed(bits_of("fsdp")):
        other = swap(held, "fsdp", bit)
        low = (index & bit) == 0
        held = jnp.stack([jnp.where(low, held, other), jnp.where(low, other, held)], axis=1)
        done *= 2
        held = held.reshape((done, rows) + rest)
    return held.reshape((done * rows,) + rest)


def reduce_group(grad):
    index = lax.axis_index("fsdp")
    count = lax.axis_size("fsdp")
    held = grad.reshape((count, grad.shape[0] // count) + grad.shape[1:])
    for bit in bits_of("fsdp"):
        left = held.shape[0] // 2
        pairs = held.reshape((left, 2) + held.shape[1:])
        low = (index & bit) == 0
        give = jnp.where(low, pairs[:, 1], pairs[:, 0]).astype(jnp.bfloat16)
        keep = jnp.where(low, pairs[:, 0], pairs[:, 1])
        held = as_float(keep) + as_float(swap(give, "fsdp", bit))
        if left > 1:
            held = held.astype(jnp.bfloat16)
    return held[0]


def reduce_replicas(value, order):
    index = lax.axis_index("rep")
    held = value
    for bit in order:
        pairs = held.reshape((2, held.shape[0] // 2) + held.shape[1:])
        low = (index & bit) == 0
        give = jnp.where(low, pairs[1], pairs[0]).astype(jnp.bfloat16)
        keep = jnp.where(low, pairs[0], pairs[1])
        held = as_float(keep) + as_float(swap(give, "rep", bit))
    held = held.astype(jnp.bfloat16)
    for bit in reversed(order):
        other = swap(held, "rep", bit)
        low = (index & bit) == 0
        held = jnp.concatenate([jnp.where(low, held, other), jnp.where(low, other, held)], axis=0)
    return as_float(held)


def total(grad):
    mine = reduce_group(grad)
    bits = bits_of("rep")
    near = bits[:2]
    order_a = bits
    order_b = near[::-1] + bits[2:]
    cut = mine.shape[1] // 2
    return jnp.concatenate(
        [reduce_replicas(mine[:, :cut], order_a), reduce_replicas(mine[:, cut:], order_b)], axis=1
    )


def body(
    tokens,
    prefix,
    cotangent,
    w_query,
    b_query,
    w_key,
    w_value,
    b_value,
    w_out,
    b_out,
    gain_one,
    shift_one,
    w_up,
    b_up,
    w_down,
    b_down,
    gain_two,
    shift_two,
):
    width = tokens.shape[1]
    vectors = [b_query, b_value, b_out, gain_one, shift_one, b_down, gain_two, shift_two, b_up]
    fsdp = lax.axis_size("fsdp")

    shard = jnp.concatenate([w_query, w_key, w_value, w_out], axis=1)
    heads_w = gather(shard)
    small = gather(jnp.concatenate(vectors)[None])
    pieces = []
    at = 0
    for vector in vectors:
        size = vector.shape[0]
        pieces.append(as_float(small[:, at : at + size].reshape(-1)))
        at += size
    b_query, b_value, b_out, gain_one, shift_one, b_down, gain_two, shift_two, b_up = pieces
    w_up = gather(w_up)
    w_down = gather(w_down)

    w_qkv = heads_w[:, : 3 * width]
    w_out = heads_w[:, 3 * width :]
    qkv = product(tokens, w_qkv)
    query = (qkv[:, :width] + b_query).astype(jnp.bfloat16)
    key = qkv[:, width : 2 * width].astype(jnp.bfloat16)
    value = (qkv[:, 2 * width :] + b_value).astype(jnp.bfloat16)
    context = attention_call(attend_kernel, prefix, (query, key, value), 1)
    attn_out = product(context, w_out) + b_out
    normed_one, inverse_one = normalize(as_float(tokens) + attn_out)
    inner = (normed_one * gain_one + shift_one).astype(jnp.bfloat16)
    upward = product(inner, w_up) + b_up
    cumulative = 0.5 * (1.0 + lax.erf(upward * 0.7071067811865476))
    active = (upward * cumulative).astype(jnp.bfloat16)
    downward = product(active, w_down) + b_down
    normed_two, inverse_two = normalize(as_float(inner) + downward)
    layer_out = (normed_two * gain_two + shift_two).astype(jnp.bfloat16)

    grad_out = as_float(cotangent)
    grad_gain_two = jnp.sum(grad_out * normed_two, axis=0)
    grad_shift_two = jnp.sum(grad_out, axis=0)
    back_two = norm_back(grad_out * gain_two, normed_two, inverse_two)
    d_down = back_two.astype(jnp.bfloat16)
    grad_b_down = jnp.sum(as_float(d_down), axis=0)
    grad_w_down = total(tn(active, d_down).astype(jnp.bfloat16))
    slope = cumulative + upward * jnp.exp(-0.5 * upward * upward) * 0.3989422804014327
    d_up = (nt(d_down, w_down) * slope).astype(jnp.bfloat16)
    grad_b_up = jnp.sum(as_float(d_up), axis=0)
    grad_w_up = total(tn(inner, d_up).astype(jnp.bfloat16))
    d_inner = nt(d_up, w_up) + back_two
    grad_gain_one = jnp.sum(d_inner * normed_one, axis=0)
    grad_shift_one = jnp.sum(d_inner, axis=0)
    back_one = norm_back(d_inner * gain_one, normed_one, inverse_one)
    d_attn = back_one.astype(jnp.bfloat16)
    grad_b_out = jnp.sum(as_float(d_attn), axis=0)
    grad_w_out = total(tn(context, d_attn).astype(jnp.bfloat16))
    d_context = nt(d_attn, w_out).astype(jnp.bfloat16)
    d_query, d_keys, d_values = attention_call(
        attend_back_kernel, prefix, (query, key, value, d_context), 3
    )
    d_qkv = jnp.concatenate([d_query, d_keys, d_values], axis=1)
    grad_qkv = total(tn(tokens, d_qkv).astype(jnp.bfloat16))
    grad_b_query = jnp.sum(as_float(d_query), axis=0)
    grad_b_value = jnp.sum(as_float(d_values), axis=0)
    token_grad = back_one + nt(d_qkv, w_qkv)

    sums = [
        grad_b_query,
        grad_b_value,
        grad_b_out,
        grad_gain_one,
        grad_shift_one,
        grad_b_down,
        grad_gain_two,
        grad_shift_two,
        grad_b_up,
    ]
    packed = jnp.concatenate([s.reshape(fsdp, -1) for s in sums], axis=1)
    small_sum = reduce_group(packed)[0]
    for bit in bits_of("rep"):
        small_sum = small_sum + swap(small_sum, "rep", bit)
    out = []
    at = 0
    for s in sums:
        size = s.shape[0] // fsdp
        out.append(small_sum[at : at + size])
        at += size
    (
        grad_b_query,
        grad_b_value,
        grad_b_out,
        grad_gain_one,
        grad_shift_one,
        grad_b_down,
        grad_gain_two,
        grad_shift_two,
        grad_b_up,
    ) = out
    return (
        layer_out,
        token_grad,
        grad_qkv[:, :width],
        grad_b_query,
        grad_qkv[:, width : 2 * width],
        grad_qkv[:, 2 * width :],
        grad_b_value,
        grad_w_out,
        grad_b_out,
        grad_gain_one,
        grad_shift_one,
        grad_w_up,
        grad_b_up,
        grad_w_down,
        grad_b_down,
        grad_gain_two,
        grad_shift_two,
    )


def solution(mesh):
    rows, flat = P(("rep", "fsdp"), None), P(("rep", "fsdp"))
    matrix, vector = P("fsdp", None), P("fsdp")
    placed = (rows, flat, rows) + (
        matrix,
        vector,
        matrix,
        matrix,
        vector,
        matrix,
        vector,
        vector,
        vector,
        matrix,
        vector,
        matrix,
        vector,
        vector,
        vector,
    )
    return jax.shard_map(
        body,
        mesh=mesh,
        in_specs=placed,
        out_specs=(rows, rows) + placed[3:],
        check_vma=False,
    )
```

```python
import functools

import jax
import jax.numpy as jnp
from jax import lax
from jax.experimental import pallas as pl
from jax.experimental.pallas import tpu as pltpu
from jax.sharding import PartitionSpec as P

H = 12
HD = 64
PAIR = 2 * HD

epsilon = 1e-12
masked_fill = -1e30

MESH = pl.DeviceIdType.MESH


def as_float(vector):
    return vector.astype(jnp.float32)


def product(left, right):
    return jnp.dot(left, right, preferred_element_type=jnp.float32)


def nt(left, right):
    return lax.dot_general(left, right, (((1,), (1,)), ((), ())), preferred_element_type=jnp.float32)


def tn(left, right):
    return lax.dot_general(left, right, (((0,), (0,)), ((), ())), preferred_element_type=jnp.float32)


def normalize(hidden):
    centre = hidden - jnp.mean(hidden, axis=-1, keepdims=True)
    inverse = lax.rsqrt(jnp.mean(centre * centre, axis=-1, keepdims=True) + epsilon)
    return (centre * inverse, inverse)


def norm_back(grad_norm, normed, inverse):
    mean_grad = jnp.mean(grad_norm, axis=-1, keepdims=True)
    mean_cross = jnp.mean(grad_norm * normed, axis=-1, keepdims=True)
    return inverse * (grad_norm - mean_grad - normed * mean_cross)


def softmax_parts(query, key, limit):
    length = query.shape[0]
    scores = nt(query, key) * HD ** (-0.5)
    row_pos = lax.broadcasted_iota(jnp.int32, (length, length), 0)
    col_pos = lax.broadcasted_iota(jnp.int32, (length, length), 1)
    visible = (col_pos <= row_pos) | (col_pos < limit)
    scores = jnp.where(visible, scores, masked_fill)
    expo = jnp.exp(scores - jnp.max(scores, axis=-1, keepdims=True))
    return expo * (1.0 / jnp.sum(expo, axis=-1, keepdims=True))


def attend_kernel(prefix_ref, q_ref, k_ref, v_ref, out_ref):
    limit = prefix_ref[pl.program_id(0)]
    outs = []
    for head in range(2):
        cols = slice(head * HD, (head + 1) * HD)
        prob = softmax_parts(q_ref[:, cols], k_ref[:, cols], limit)
        outs.append(product(prob.astype(jnp.bfloat16), v_ref[:, cols]))
    out_ref[...] = jnp.concatenate(outs, axis=1).astype(jnp.bfloat16)


def attend_back_pair(query, key, value, d_context, limit):
    d_q, d_k, d_v = [], [], []
    for head in range(2):
        cols = slice(head * HD, (head + 1) * HD)
        q, k, v, d = query[:, cols], key[:, cols], value[:, cols], d_context[:, cols]
        prob = softmax_parts(q, k, limit)
        d_v.append(tn(prob.astype(jnp.bfloat16), d))
        d_prob = as_float(nt(d, v).astype(jnp.bfloat16))
        weighted = prob * d_prob
        d_scores = (weighted - prob * jnp.sum(weighted, axis=-1, keepdims=True)).astype(jnp.bfloat16)
        d_q.append(product(d_scores, k) * HD ** (-0.5))
        d_k.append(tn(d_scores, q) * HD ** (-0.5))
    return [jnp.concatenate(p, axis=1).astype(jnp.bfloat16) for p in (d_q, d_k, d_v)]


def attend_back_kernel(prefix_ref, q_ref, k_ref, v_ref, d_ref, dq_ref, dk_ref, dv_ref):
    limit = prefix_ref[pl.program_id(0)]
    parts = attend_back_pair(q_ref[...], k_ref[...], v_ref[...], d_ref[...], limit)
    for ref, part in zip((dq_ref, dk_ref, dv_ref), parts):
        ref[...] = part


def attention_call(kernel, prefix, operands, outputs):
    rows, width = operands[0].shape
    length = rows // prefix.shape[0]
    block = pl.BlockSpec((length, PAIR), lambda s, h, p: (s, h))
    shape = jax.ShapeDtypeStruct((rows, width), jnp.bfloat16)
    single = outputs == 1
    return pl.pallas_call(
        kernel,
        out_shape=shape if single else [shape] * outputs,
        grid_spec=pltpu.PrefetchScalarGridSpec(
            num_scalar_prefetch=1,
            grid=(prefix.shape[0], width // PAIR),
            in_specs=[block] * len(operands),
            out_specs=block if single else [block] * outputs,
        ),
        cost_estimate=pl.CostEstimate(
            flops=4 * len(operands) * rows * length * width,
            bytes_accessed=2 * rows * width * (len(operands) + outputs),
            transcendentals=rows * length * H,
        ),
    )(prefix, *operands)


def swap(value, axis, bit):
    size = lax.axis_size(axis)
    return lax.ppermute(value, axis, [(i, i ^ bit) for i in range(size)])


def bits_of(axis):
    size = lax.axis_size(axis)
    assert size & (size - 1) == 0
    return [1 << b for b in range(size.bit_length() - 1)]


def gather(block):
    index = lax.axis_index("fsdp")
    rows = block.shape[0]
    rest = block.shape[1:]
    held = block.reshape((1, rows) + rest)
    done = 1
    for bit in reversed(bits_of("fsdp")):
        other = swap(held, "fsdp", bit)
        low = (index & bit) == 0
        held = jnp.stack([jnp.where(low, held, other), jnp.where(low, other, held)], axis=1)
        done *= 2
        held = held.reshape((done, rows) + rest)
    return held.reshape((done * rows,) + rest)


def reduce_group(grad):
    index = lax.axis_index("fsdp")
    count = lax.axis_size("fsdp")
    held = grad.reshape((count, grad.shape[0] // count) + grad.shape[1:])
    for bit in bits_of("fsdp"):
        left = held.shape[0] // 2
        pairs = held.reshape((left, 2) + held.shape[1:])
        low = (index & bit) == 0
        give = jnp.where(low, pairs[:, 1], pairs[:, 0]).astype(jnp.bfloat16)
        keep = jnp.where(low, pairs[:, 0], pairs[:, 1])
        held = as_float(keep) + as_float(swap(give, "fsdp", bit))
        if left > 1:
            held = held.astype(jnp.bfloat16)
    return held[0]


def reduce_replicas(value, order):
    index = lax.axis_index("rep")
    held = value
    for bit in order:
        pairs = held.reshape((2, held.shape[0] // 2) + held.shape[1:])
        low = (index & bit) == 0
        give = jnp.where(low, pairs[1], pairs[0]).astype(jnp.bfloat16)
        keep = jnp.where(low, pairs[0], pairs[1])
        held = as_float(keep) + as_float(swap(give, "rep", bit))
    held = held.astype(jnp.bfloat16)
    for bit in reversed(order):
        other = swap(held, "rep", bit)
        low = (index & bit) == 0
        held = jnp.concatenate([jnp.where(low, held, other), jnp.where(low, other, held)], axis=0)
    return as_float(held)


def total(grad):
    mine = reduce_group(grad)
    bits = bits_of("rep")
    near = bits[:2]
    order_a = bits
    order_b = near[::-1] + bits[2:]
    cut = mine.shape[1] // 2
    return jnp.concatenate(
        [reduce_replicas(mine[:, :cut], order_a), reduce_replicas(mine[:, cut:], order_b)], axis=1
    )


def reduce_kernel(prefix_ref, active_ref, d_down_ref, inner_ref, d_up_ref, context_ref, d_attn_ref, tokens_ref,
                  q_ref, k_ref, v_ref, d_context_ref, small_ref, out_ref, d_qkv_ref, small_out,
                  g_ref, core_in, x_out, x_in, in_one, in_two, in_three, res, v_held, v_in,
                  send, recv, v_send, v_recv):
    rep, fsdp = lax.axis_index("rep"), lax.axis_index("fsdp")
    core, side = lax.rem(fsdp, 2), fsdp // 2
    chunks = res.shape[0]

    def flip(index, bit):
        return index + bit * (1 - 2 * lax.rem(index // bit, 2))

    sibling = (rep, flip(fsdp, 1))
    across = (rep, flip(fsdp, 2))
    barrier = pltpu.get_barrier_semaphore()
    partners = [sibling, across] + [(flip(rep, bit), fsdp) for bit in (1, 2, 4)]
    for partner in partners:
        pl.semaphore_signal(barrier, inc=1, device_id=partner, device_id_type=MESH)
    pl.semaphore_wait(barrier, len(partners))

    def turns(k):
        first = 1 + lax.rem(k, 2)
        second = 3 - first
        return [(flip(rep, b), lax.rem(rep // b, 2)) for b in (first, second, 4)]

    def copies(k, stage):
        (p_one, m_one), (p_two, m_two), (p_three, m_three) = turns(k)
        rows = x_in.shape[2]
        half, quarter = rows // 2, rows // 4
        mine_two = pl.ds(pl.multiple_of(m_two * half, half), half)
        away_two = pl.ds(pl.multiple_of((1 - m_two) * half, half), half)
        away_three = pl.ds(pl.multiple_of((1 - m_three) * quarter, quarter), quarter)
        piece = pl.ds(pl.multiple_of(m_two * half + m_three * quarter, quarter), quarter)
        if stage == 0:
            src, dst, to = g_ref.at[k, 1 - core], core_in.at[k], sibling
        elif stage == 1:
            src, dst, to = x_out.at[k], x_in.at[k], across
        elif stage == 2:
            src, dst, to = x_in.at[k, 1 - m_one], in_one.at[k], (p_one, fsdp)
        elif stage == 3:
            src, dst, to = in_one.at[k, away_two], in_two.at[k], (p_two, fsdp)
        elif stage == 4:
            src, dst, to = in_two.at[k, away_three], in_three.at[k], (p_three, fsdp)
        elif stage == 5:
            src, dst, to = res.at[k, m_one, piece], res.at[k, m_one, piece], (p_three, fsdp)
        elif stage == 6:
            src, dst, to = res.at[k, m_one, mine_two], res.at[k, m_one, mine_two], (p_two, fsdp)
        else:
            src, dst, to = res.at[k, m_one], res.at[k, m_one], (p_one, fsdp)
        return pltpu.make_async_remote_copy(
            src_ref=src, dst_ref=dst, send_sem=send.at[stage, k], recv_sem=recv.at[stage, k],
            device_id=to, device_id_type=MESH)

    def step(k, stage):
        (_, m_one), (_, m_two), (_, m_three) = turns(k)
        rows = x_in.shape[2]
        half, quarter = rows // 2, rows // 4
        if stage >= 0:
            copies(k, stage).wait_recv()
        if stage == 0:
            x_out[k] = (as_float(g_ref[k, core, 1 - side]) + as_float(core_in[k, 1 - side])).astype(jnp.bfloat16)
        elif stage == 1:
            x_in[k] = (as_float(g_ref[k, core, side]) + as_float(core_in[k, side]) + as_float(x_in[k])).astype(jnp.bfloat16)
        elif stage == 2:
            in_one[k] = (as_float(x_in[k, m_one]) + as_float(in_one[k])).astype(jnp.bfloat16)
        elif stage == 3:
            at = pl.ds(pl.multiple_of(m_two * half, half), half)
            in_two[k] = (as_float(in_one[k, at]) + as_float(in_two[k])).astype(jnp.bfloat16)
        elif stage == 4:
            at = pl.ds(pl.multiple_of(m_three * quarter, quarter), quarter)
            piece = pl.ds(pl.multiple_of(m_two * half + m_three * quarter, quarter), quarter)
            res[k, m_one, piece] = (as_float(in_two[k, at]) + as_float(in_three[k])).astype(jnp.bfloat16)
        elif stage == 7:
            out_ref[k] = res[k]
        if stage < 7:
            copies(k, stage + 1).start()

    width = tokens_ref.shape[1]

    def v_copy(i):
        to = [sibling, across, (flip(rep, 1), fsdp), (flip(rep, 2), fsdp), (flip(rep, 4), fsdp)][i]
        return pltpu.make_async_remote_copy(
            src_ref=v_held.at[i], dst_ref=v_in.at[i], send_sem=v_send.at[i], recv_sem=v_recv.at[i],
            device_id=to, device_id_type=MESH)

    def v_step(i):
        if i == 0:
            v_held[0] = small_ref[...]
            for row, part in ((0, 0), (1, 2)):
                columns = as_float(d_qkv_ref[:, part * width : (part + 1) * width])
                v_held[0, row : row + 1, :] = jnp.sum(columns, axis=0, keepdims=True)
        else:
            v_copy(i - 1).wait_recv()
            total_now = v_held[i - 1] + v_in[i - 1]
            if i < 5:
                v_held[i] = total_now
            else:
                small_out[...] = total_now
        if i < 5:
            v_copy(i).start()

    def store_columns(k, half, value):
        rows = res.shape[2]
        for x in range(2):
            for c in range(2):
                at = (2 * x + c) * rows
                g_ref[k, c, x, half] = value[at : at + rows].astype(jnp.bfloat16)

    cut = width // 2

    def make(k):
        rows = res.shape[2]

        @pl.when(k < 4)
        def _():
            right = d_down_ref[:, pl.ds(pl.multiple_of(lax.rem(k, 2) * cut, cut), cut)]
            for x in range(2):
                for c in range(2):
                    at = (2 * x + c) * width + (k // 2) * cut
                    value = tn(active_ref[:, pl.ds(pl.multiple_of(at, cut), cut)], right)
                    g_ref[k, c, x, 0] = value[:rows].astype(jnp.bfloat16)
                    g_ref[k, c, x, 1] = value[rows:].astype(jnp.bfloat16)

        @pl.when((k >= 4) & (k < 8))
        def _():
            for half in range(2):
                at = pl.multiple_of((k - 4) * width + half * cut, cut)
                store_columns(k, half, tn(inner_ref[...], d_up_ref[:, pl.ds(at, cut)]))

        @pl.when(k == 8)
        def _():
            for half in range(2):
                store_columns(k, half, tn(context_ref[...], d_attn_ref[:, half * cut : (half + 1) * cut]))

        @pl.when(k >= 9)
        def _():
            for half in range(2):
                at = pl.multiple_of((k - 9) * width + half * cut, cut)
                store_columns(k, half, tn(tokens_ref[...], d_qkv_ref[:, pl.ds(at, cut)]))

    pairs = width // PAIR
    length = tokens_ref.shape[0] // prefix_ref.shape[0]
    units = prefix_ref.shape[0] * pairs

    def attend_back(unit):
        sequence, pair = unit // pairs, lax.rem(unit, pairs)
        here = pl.ds(pl.multiple_of(sequence * length, length), length)
        at = pl.multiple_of(pair * PAIR, PAIR)
        limit = prefix_ref[sequence]
        query, key, value, d_context = [ref[here, pl.ds(at, PAIR)] for ref in (q_ref, k_ref, v_ref, d_context_ref)]
        parts = attend_back_pair(query, key, value, d_context, limit)
        for part in range(3):
            d_qkv_ref[here, pl.ds(pl.multiple_of(part * width + at, PAIR), PAIR)] = parts[part]

    lead = 2

    def tick(t, carry):
        for stage in range(-1, 8):
            k = t + (lead if stage == -1 else 1 - stage)

            @pl.when((k >= 0) & (k < chunks))
            def _():
                if stage == -1:
                    make(k)
                step(k, stage)

        @pl.when((t >= 0) & (t < units // 2))
        def _():
            attend_back(2 * t)
            attend_back(2 * t + 1)

        for i in range(6):
            @pl.when(t == units // 2 + i)
            def _():
                v_step(i)
        return carry

    lax.fori_loop(-lead, chunks + 6, tick, 0)

    def drain(k, carry):
        for stage in range(8):
            copies(k, stage).wait_send()
        return carry

    lax.fori_loop(0, chunks, drain, 0)
    for i in range(5):
        v_copy(i).wait_send()


def reduce_call(prefix, *operands):
    active, d_down, inner, d_up, context, d_attn, tokens, query, key, value, d_context, small = operands
    tokens_here, width = tokens.shape
    chunks, rows, columns = 12, width // 4, width // 2
    low = jnp.bfloat16

    def buf(*shape):
        return pltpu.VMEM((chunks,) + shape, low)

    dma = pltpu.SemaphoreType.DMA
    vmem = pl.BlockSpec(memory_space=pltpu.VMEM)
    return pl.pallas_call(
        reduce_kernel,
        out_shape=(
            jax.ShapeDtypeStruct((chunks, 2, rows, columns), low),
            jax.ShapeDtypeStruct((tokens_here, 3 * width), low),
            jax.ShapeDtypeStruct(small.shape, jnp.float32),
        ),
        in_specs=[pl.BlockSpec(memory_space=pltpu.SMEM)] + [vmem] * len(operands),
        out_specs=(vmem,) * 3,
        scratch_shapes=[
            buf(2, 2, 2, rows, columns),
            buf(2, 2, rows, columns),
            buf(2, rows, columns),
            buf(2, rows, columns),
            buf(rows, columns),
            buf(rows // 2, columns),
            buf(rows // 4, columns),
            buf(2, rows, columns),
            pltpu.VMEM((5,) + small.shape, jnp.float32),
            pltpu.VMEM((5,) + small.shape, jnp.float32),
            dma((8, chunks)),
            dma((8, chunks)),
            dma((5,)),
            dma((5,)),
        ],
        compiler_params=pltpu.CompilerParams(
            collective_id=1, has_side_effects=True, vmem_limit_bytes=63_000_000
        ),
    )(prefix, *operands)


def body(
    tokens,
    prefix,
    cotangent,
    w_query,
    b_query,
    w_key,
    w_value,
    b_value,
    w_out,
    b_out,
    gain_one,
    shift_one,
    w_up,
    b_up,
    w_down,
    b_down,
    gain_two,
    shift_two,
):
    width = tokens.shape[1]
    vectors = [b_query, b_value, b_out, gain_one, shift_one, b_down, gain_two, shift_two, b_up]
    fsdp = lax.axis_size("fsdp")

    shard = jnp.concatenate([w_query, w_key, w_value, w_out], axis=1)
    heads_w = gather(shard)
    small = gather(jnp.concatenate(vectors)[None])
    pieces = []
    at = 0
    for vector in vectors:
        size = vector.shape[0]
        pieces.append(as_float(small[:, at : at + size].reshape(-1)))
        at += size
    b_query, b_value, b_out, gain_one, shift_one, b_down, gain_two, shift_two, b_up = pieces
    w_up = gather(w_up)
    w_down = gather(w_down)

    w_qkv = heads_w[:, : 3 * width]
    w_out = heads_w[:, 3 * width :]
    qkv = product(tokens, w_qkv)
    query = (qkv[:, :width] + b_query).astype(jnp.bfloat16)
    key = qkv[:, width : 2 * width].astype(jnp.bfloat16)
    value = (qkv[:, 2 * width :] + b_value).astype(jnp.bfloat16)
    context = attention_call(attend_kernel, prefix, (query, key, value), 1)
    attn_out = product(context, w_out) + b_out
    normed_one, inverse_one = normalize(as_float(tokens) + attn_out)
    inner = (normed_one * gain_one + shift_one).astype(jnp.bfloat16)
    upward = product(inner, w_up) + b_up
    cumulative = 0.5 * (1.0 + lax.erf(upward * 0.7071067811865476))
    active = (upward * cumulative).astype(jnp.bfloat16)
    downward = product(active, w_down) + b_down
    normed_two, inverse_two = normalize(as_float(inner) + downward)
    layer_out = (normed_two * gain_two + shift_two).astype(jnp.bfloat16)

    grad_out = as_float(cotangent)
    grad_gain_two = jnp.sum(grad_out * normed_two, axis=0)
    grad_shift_two = jnp.sum(grad_out, axis=0)
    back_two = norm_back(grad_out * gain_two, normed_two, inverse_two)
    d_down = back_two.astype(jnp.bfloat16)
    grad_b_down = jnp.sum(as_float(d_down), axis=0)
    slope = cumulative + upward * jnp.exp(-0.5 * upward * upward) * 0.3989422804014327
    d_up = (nt(d_down, w_down) * slope).astype(jnp.bfloat16)
    grad_b_up = jnp.sum(as_float(d_up), axis=0)
    d_inner = nt(d_up, w_up) + back_two
    grad_gain_one = jnp.sum(d_inner * normed_one, axis=0)
    grad_shift_one = jnp.sum(d_inner, axis=0)
    back_one = norm_back(d_inner * gain_one, normed_one, inverse_one)
    d_attn = back_one.astype(jnp.bfloat16)
    grad_b_out = jnp.sum(as_float(d_attn), axis=0)
    d_context = nt(d_attn, w_out).astype(jnp.bfloat16)
    sums = [grad_b_out, grad_gain_one, grad_shift_one, grad_b_down, grad_gain_two, grad_shift_two, grad_b_up]
    if lax.axis_size("fsdp") == 4 and lax.axis_size("rep") == 8:
        none = jnp.zeros((width,), jnp.float32)
        packed = jnp.concatenate([none, none] + sums + [none] * 4).reshape(-1, width)
        chunked, d_qkv, packed = reduce_call(
            prefix, active, d_down, inner, d_up, context, d_attn, tokens, query, key, value, d_context, packed
        )
        rows = chunked.shape[2]
        grad_w_down = chunked[:4].reshape(2, 2, 2, rows, -1).transpose(0, 2, 3, 1, 4).reshape(4 * rows, width)
        wide = chunked[4:].transpose(2, 0, 1, 3).reshape(rows, 8 * width)
        grad_w_up = wide[:, : 4 * width]
        grad_w_out = wide[:, 4 * width : 5 * width]
        grad_qkv = wide[:, 5 * width :]
        packed = packed.reshape(-1)
        mine = lax.axis_index("fsdp")
        vectors, at = [], 0
        for size in [width] * 8 + [4 * width]:
            block = size // fsdp
            vectors.append(lax.dynamic_slice_in_dim(packed, at + mine * block, block))
            at += size
    else:
        grad_w_down = total(tn(active, d_down).astype(jnp.bfloat16))
        grad_w_up = total(tn(inner, d_up).astype(jnp.bfloat16))
        grad_w_out = total(tn(context, d_attn).astype(jnp.bfloat16))
        d_query, d_keys, d_values = attention_call(
            attend_back_kernel, prefix, (query, key, value, d_context), 3
        )
        d_qkv = jnp.concatenate([d_query, d_keys, d_values], axis=1)
        grad_qkv = total(tn(tokens, d_qkv).astype(jnp.bfloat16))
        sums = [jnp.sum(as_float(d_query), axis=0), jnp.sum(as_float(d_values), axis=0)] + sums
        packed = jnp.concatenate([s.reshape(fsdp, -1) for s in sums], axis=1)
        small_sum = reduce_group(packed)[0]
        for bit in bits_of("rep"):
            small_sum = small_sum + swap(small_sum, "rep", bit)
        vectors, at = [], 0
        for s in sums:
            size = s.shape[0] // fsdp
            vectors.append(small_sum[at : at + size])
            at += size
    token_grad = back_one + nt(d_qkv, w_qkv)
    (
        grad_b_query,
        grad_b_value,
        grad_b_out,
        grad_gain_one,
        grad_shift_one,
        grad_b_down,
        grad_gain_two,
        grad_shift_two,
        grad_b_up,
    ) = vectors
    grad_qkv, grad_w_out, grad_w_up, grad_w_down = [
        as_float(g) for g in (grad_qkv, grad_w_out, grad_w_up, grad_w_down)
    ]
    return (
        layer_out,
        token_grad,
        grad_qkv[:, :width],
        grad_b_query,
        grad_qkv[:, width : 2 * width],
        grad_qkv[:, 2 * width :],
        grad_b_value,
        grad_w_out,
        grad_b_out,
        grad_gain_one,
        grad_shift_one,
        grad_w_up,
        grad_b_up,
        grad_w_down,
        grad_b_down,
        grad_gain_two,
        grad_shift_two,
    )


def solution(mesh):
    rows, flat = P(("rep", "fsdp"), None), P(("rep", "fsdp"))
    matrix, vector = P("fsdp", None), P("fsdp")
    placed = (rows, flat, rows) + (
        matrix,
        vector,
        matrix,
        matrix,
        vector,
        matrix,
        vector,
        vector,
        vector,
        matrix,
        vector,
        matrix,
        vector,
        vector,
        vector,
    )
    return jax.shard_map(
        body,
        mesh=mesh,
        in_specs=placed,
        out_specs=(rows, rows) + placed[3:],
        check_vma=False,
    )
```

```python
import functools

import jax
import jax.numpy as jnp
from jax import lax
from jax.experimental import pallas as pl
from jax.experimental.pallas import tpu as pltpu
from jax.sharding import PartitionSpec as P

H = 12
HD = 64
PAIR = 2 * HD

epsilon = 1e-12
masked_fill = -1e30

MESH = pl.DeviceIdType.MESH


def as_float(vector):
    return vector.astype(jnp.float32)


def product(left, right):
    return jnp.dot(left, right, preferred_element_type=jnp.float32)


def nt(left, right):
    return lax.dot_general(left, right, (((1,), (1,)), ((), ())), preferred_element_type=jnp.float32)


def tn(left, right):
    return lax.dot_general(left, right, (((0,), (0,)), ((), ())), preferred_element_type=jnp.float32)


def normalize(hidden):
    centre = hidden - jnp.mean(hidden, axis=-1, keepdims=True)
    inverse = lax.rsqrt(jnp.mean(centre * centre, axis=-1, keepdims=True) + epsilon)
    return (centre * inverse, inverse)


def norm_back(grad_norm, normed, inverse):
    mean_grad = jnp.mean(grad_norm, axis=-1, keepdims=True)
    mean_cross = jnp.mean(grad_norm * normed, axis=-1, keepdims=True)
    return inverse * (grad_norm - mean_grad - normed * mean_cross)


def softmax_parts(query, key, limit):
    length = query.shape[0]
    scores = nt(query, key) * HD ** (-0.5)
    row_pos = lax.broadcasted_iota(jnp.int32, (length, length), 0)
    col_pos = lax.broadcasted_iota(jnp.int32, (length, length), 1)
    visible = (col_pos <= row_pos) | (col_pos < limit)
    scores = jnp.where(visible, scores, masked_fill)
    expo = jnp.exp(scores - jnp.max(scores, axis=-1, keepdims=True))
    return expo * (1.0 / jnp.sum(expo, axis=-1, keepdims=True))


def attend_pair(query, key, value, limit):
    outs = []
    for head in range(2):
        cols = slice(head * HD, (head + 1) * HD)
        prob = softmax_parts(query[:, cols], key[:, cols], limit)
        outs.append(product(prob.astype(jnp.bfloat16), value[:, cols]))
    return jnp.concatenate(outs, axis=1).astype(jnp.bfloat16)


def attend_kernel(prefix_ref, q_ref, k_ref, v_ref, out_ref):
    limit = prefix_ref[pl.program_id(0)]
    out_ref[...] = attend_pair(q_ref[...], k_ref[...], v_ref[...], limit)


def attend_back_pair(query, key, value, d_context, limit):
    d_q, d_k, d_v = [], [], []
    for head in range(2):
        cols = slice(head * HD, (head + 1) * HD)
        q, k, v, d = query[:, cols], key[:, cols], value[:, cols], d_context[:, cols]
        prob = softmax_parts(q, k, limit)
        d_v.append(tn(prob.astype(jnp.bfloat16), d))
        d_prob = as_float(nt(d, v).astype(jnp.bfloat16))
        weighted = prob * d_prob
        d_scores = (weighted - prob * jnp.sum(weighted, axis=-1, keepdims=True)).astype(jnp.bfloat16)
        d_q.append(product(d_scores, k) * HD ** (-0.5))
        d_k.append(tn(d_scores, q) * HD ** (-0.5))
    return [jnp.concatenate(p, axis=1).astype(jnp.bfloat16) for p in (d_q, d_k, d_v)]


def attend_back_kernel(prefix_ref, q_ref, k_ref, v_ref, d_ref, dq_ref, dk_ref, dv_ref):
    limit = prefix_ref[pl.program_id(0)]
    parts = attend_back_pair(q_ref[...], k_ref[...], v_ref[...], d_ref[...], limit)
    for ref, part in zip((dq_ref, dk_ref, dv_ref), parts):
        ref[...] = part


def attention_call(kernel, prefix, operands, outputs):
    rows, width = operands[0].shape
    length = rows // prefix.shape[0]
    block = pl.BlockSpec((length, PAIR), lambda s, h, p: (s, h))
    shape = jax.ShapeDtypeStruct((rows, width), jnp.bfloat16)
    single = outputs == 1
    return pl.pallas_call(
        kernel,
        out_shape=shape if single else [shape] * outputs,
        grid_spec=pltpu.PrefetchScalarGridSpec(
            num_scalar_prefetch=1,
            grid=(prefix.shape[0], width // PAIR),
            in_specs=[block] * len(operands),
            out_specs=block if single else [block] * outputs,
        ),
        cost_estimate=pl.CostEstimate(
            flops=4 * len(operands) * rows * length * width,
            bytes_accessed=2 * rows * width * (len(operands) + outputs),
            transcendentals=rows * length * H,
        ),
    )(prefix, *operands)


def swap(value, axis, bit):
    size = lax.axis_size(axis)
    return lax.ppermute(value, axis, [(i, i ^ bit) for i in range(size)])


def bits_of(axis):
    size = lax.axis_size(axis)
    assert size & (size - 1) == 0
    return [1 << b for b in range(size.bit_length() - 1)]


def gather(block):
    index = lax.axis_index("fsdp")
    rows = block.shape[0]
    rest = block.shape[1:]
    held = block.reshape((1, rows) + rest)
    done = 1
    for bit in reversed(bits_of("fsdp")):
        other = swap(held, "fsdp", bit)
        low = (index & bit) == 0
        held = jnp.stack([jnp.where(low, held, other), jnp.where(low, other, held)], axis=1)
        done *= 2
        held = held.reshape((done, rows) + rest)
    return held.reshape((done * rows,) + rest)


def reduce_group(grad):
    index = lax.axis_index("fsdp")
    count = lax.axis_size("fsdp")
    held = grad.reshape((count, grad.shape[0] // count) + grad.shape[1:])
    for bit in bits_of("fsdp"):
        left = held.shape[0] // 2
        pairs = held.reshape((left, 2) + held.shape[1:])
        low = (index & bit) == 0
        give = jnp.where(low, pairs[:, 1], pairs[:, 0]).astype(jnp.bfloat16)
        keep = jnp.where(low, pairs[:, 0], pairs[:, 1])
        held = as_float(keep) + as_float(swap(give, "fsdp", bit))
        if left > 1:
            held = held.astype(jnp.bfloat16)
    return held[0]


def reduce_replicas(value, order):
    index = lax.axis_index("rep")
    held = value
    for bit in order:
        pairs = held.reshape((2, held.shape[0] // 2) + held.shape[1:])
        low = (index & bit) == 0
        give = jnp.where(low, pairs[1], pairs[0]).astype(jnp.bfloat16)
        keep = jnp.where(low, pairs[0], pairs[1])
        held = as_float(keep) + as_float(swap(give, "rep", bit))
    held = held.astype(jnp.bfloat16)
    for bit in reversed(order):
        other = swap(held, "rep", bit)
        low = (index & bit) == 0
        held = jnp.concatenate([jnp.where(low, held, other), jnp.where(low, other, held)], axis=0)
    return as_float(held)


def total(grad):
    mine = reduce_group(grad)
    bits = bits_of("rep")
    near = bits[:2]
    order_a = bits
    order_b = near[::-1] + bits[2:]
    cut = mine.shape[1] // 2
    return jnp.concatenate(
        [reduce_replicas(mine[:, :cut], order_a), reduce_replicas(mine[:, cut:], order_b)], axis=1
    )


def reduce_kernel(prefix_ref, active_ref, d_down_ref, inner_ref, d_up_ref, context_ref, d_attn_ref, tokens_ref,
                  qkv_ref, d_context_ref, small_ref, out_ref, d_qkv_ref, small_out,
                  g_ref, core_in, x_out, x_in, in_one, in_two, in_three, res, v_held, v_in,
                  send, recv, v_send, v_recv):
    rep, fsdp = lax.axis_index("rep"), lax.axis_index("fsdp")
    core, side = lax.rem(fsdp, 2), fsdp // 2
    chunks = res.shape[0]

    def flip(index, bit):
        return index + bit * (1 - 2 * lax.rem(index // bit, 2))

    sibling = (rep, flip(fsdp, 1))
    across = (rep, flip(fsdp, 2))
    barrier = pltpu.get_barrier_semaphore()
    partners = [sibling, across] + [(flip(rep, bit), fsdp) for bit in (1, 2, 4)]
    for partner in partners:
        pl.semaphore_signal(barrier, inc=1, device_id=partner, device_id_type=MESH)
    pl.semaphore_wait(barrier, len(partners))

    def turns(k):
        first = 1 + lax.rem(k, 2)
        second = 3 - first
        return [(flip(rep, b), lax.rem(rep // b, 2)) for b in (first, second, 4)]

    def copies(k, stage):
        (p_one, m_one), (p_two, m_two), (p_three, m_three) = turns(k)
        rows = x_in.shape[2]
        half, quarter = rows // 2, rows // 4
        mine_two = pl.ds(pl.multiple_of(m_two * half, half), half)
        away_two = pl.ds(pl.multiple_of((1 - m_two) * half, half), half)
        away_three = pl.ds(pl.multiple_of((1 - m_three) * quarter, quarter), quarter)
        piece = pl.ds(pl.multiple_of(m_two * half + m_three * quarter, quarter), quarter)
        if stage == 0:
            src, dst, to = g_ref.at[k, 1 - core], core_in.at[k], sibling
        elif stage == 1:
            src, dst, to = x_out.at[k], x_in.at[k], across
        elif stage == 2:
            src, dst, to = x_in.at[k, 1 - m_one], in_one.at[k], (p_one, fsdp)
        elif stage == 3:
            src, dst, to = in_one.at[k, away_two], in_two.at[k], (p_two, fsdp)
        elif stage == 4:
            src, dst, to = in_two.at[k, away_three], in_three.at[k], (p_three, fsdp)
        elif stage == 5:
            src, dst, to = res.at[k, m_one, piece], res.at[k, m_one, piece], (p_three, fsdp)
        elif stage == 6:
            src, dst, to = res.at[k, m_one, mine_two], res.at[k, m_one, mine_two], (p_two, fsdp)
        else:
            src, dst, to = res.at[k, m_one], res.at[k, m_one], (p_one, fsdp)
        return pltpu.make_async_remote_copy(
            src_ref=src, dst_ref=dst, send_sem=send.at[stage, k], recv_sem=recv.at[stage, k],
            device_id=to, device_id_type=MESH)

    def step(k, stage):
        (_, m_one), (_, m_two), (_, m_three) = turns(k)
        rows = x_in.shape[2]
        half, quarter = rows // 2, rows // 4
        if stage >= 0:
            copies(k, stage).wait_recv()
        if stage == 0:
            x_out[k] = (as_float(g_ref[k, core, 1 - side]) + as_float(core_in[k, 1 - side])).astype(jnp.bfloat16)
        elif stage == 1:
            x_in[k] = (as_float(g_ref[k, core, side]) + as_float(core_in[k, side]) + as_float(x_in[k])).astype(jnp.bfloat16)
        elif stage == 2:
            in_one[k] = (as_float(x_in[k, m_one]) + as_float(in_one[k])).astype(jnp.bfloat16)
        elif stage == 3:
            at = pl.ds(pl.multiple_of(m_two * half, half), half)
            in_two[k] = (as_float(in_one[k, at]) + as_float(in_two[k])).astype(jnp.bfloat16)
        elif stage == 4:
            at = pl.ds(pl.multiple_of(m_three * quarter, quarter), quarter)
            piece = pl.ds(pl.multiple_of(m_two * half + m_three * quarter, quarter), quarter)
            res[k, m_one, piece] = (as_float(in_two[k, at]) + as_float(in_three[k])).astype(jnp.bfloat16)
        elif stage == 7:
            out_ref[k] = res[k]
        if stage < 7:
            copies(k, stage + 1).start()

    width = tokens_ref.shape[1]

    def v_copy(i):
        to = [sibling, across, (flip(rep, 1), fsdp), (flip(rep, 2), fsdp), (flip(rep, 4), fsdp)][i]
        return pltpu.make_async_remote_copy(
            src_ref=v_held.at[i], dst_ref=v_in.at[i], send_sem=v_send.at[i], recv_sem=v_recv.at[i],
            device_id=to, device_id_type=MESH)

    def v_step(i):
        if i == 0:
            v_held[0] = small_ref[...]
            for row, part in ((0, 0), (1, 2)):
                columns = as_float(d_qkv_ref[:, part * width : (part + 1) * width])
                v_held[0, row : row + 1, :] = jnp.sum(columns, axis=0, keepdims=True)
        else:
            v_copy(i - 1).wait_recv()
            total_now = v_held[i - 1] + v_in[i - 1]
            if i < 5:
                v_held[i] = total_now
            else:
                small_out[...] = total_now
        if i < 5:
            v_copy(i).start()

    def store_columns(k, half, value):
        rows = res.shape[2]
        for x in range(2):
            for c in range(2):
                at = (2 * x + c) * rows
                g_ref[k, c, x, half] = value[at : at + rows].astype(jnp.bfloat16)

    cut = width // 2

    def make(k):
        rows = res.shape[2]

        @pl.when(k < 4)
        def _():
            right = d_down_ref[:, pl.ds(pl.multiple_of(lax.rem(k, 2) * cut, cut), cut)]
            for x in range(2):
                for c in range(2):
                    at = (2 * x + c) * width + (k // 2) * cut
                    value = tn(active_ref[:, pl.ds(pl.multiple_of(at, cut), cut)], right)
                    g_ref[k, c, x, 0] = value[:rows].astype(jnp.bfloat16)
                    g_ref[k, c, x, 1] = value[rows:].astype(jnp.bfloat16)

        @pl.when((k >= 4) & (k < 8))
        def _():
            for half in range(2):
                at = pl.multiple_of((k - 4) * width + half * cut, cut)
                store_columns(k, half, tn(inner_ref[...], d_up_ref[:, pl.ds(at, cut)]))

        @pl.when(k == 8)
        def _():
            for half in range(2):
                store_columns(k, half, tn(context_ref[...], d_attn_ref[:, half * cut : (half + 1) * cut]))

        @pl.when(k >= 9)
        def _():
            for half in range(2):
                at = pl.multiple_of((k - 9) * width + half * cut, cut)
                store_columns(k, half, tn(tokens_ref[...], d_qkv_ref[:, pl.ds(at, cut)]))

    pairs = width // PAIR
    length = tokens_ref.shape[0] // prefix_ref.shape[0]
    units = prefix_ref.shape[0] * pairs

    def attend_back(unit):
        sequence, pair = unit // pairs, lax.rem(unit, pairs)
        here = pl.ds(pl.multiple_of(sequence * length, length), length)
        at = pl.multiple_of(pair * PAIR, PAIR)
        limit = prefix_ref[sequence]
        query, key, value = [qkv_ref[part, here, pl.ds(at, PAIR)] for part in range(3)]
        d_context = d_context_ref[here, pl.ds(at, PAIR)]
        parts = attend_back_pair(query, key, value, d_context, limit)
        for part in range(3):
            d_qkv_ref[here, pl.ds(pl.multiple_of(part * width + at, PAIR), PAIR)] = parts[part]

    lead = 2

    def tick(t, carry):
        for stage in range(-1, 8):
            k = t + (lead if stage == -1 else 1 - stage)

            @pl.when((k >= 0) & (k < chunks))
            def _():
                if stage == -1:
                    make(k)
                step(k, stage)

        @pl.when((t >= 0) & (t < units // 2))
        def _():
            attend_back(2 * t)
            attend_back(2 * t + 1)

        for i in range(6):
            @pl.when(t == units // 2 + i)
            def _():
                v_step(i)
        return carry

    lax.fori_loop(-lead, chunks + 6, tick, 0)

    def drain(k, carry):
        for stage in range(8):
            copies(k, stage).wait_send()
        return carry

    lax.fori_loop(0, chunks, drain, 0)
    for i in range(5):
        v_copy(i).wait_send()


def reduce_call(prefix, *operands):
    active, d_down, inner, d_up, context, d_attn, tokens, qkv, d_context, small = operands
    tokens_here, width = tokens.shape
    chunks, rows, columns = 12, width // 4, width // 2
    low = jnp.bfloat16

    def buf(*shape):
        return pltpu.VMEM((chunks,) + shape, low)

    dma = pltpu.SemaphoreType.DMA
    vmem = pl.BlockSpec(memory_space=pltpu.VMEM)
    return pl.pallas_call(
        reduce_kernel,
        out_shape=(
            jax.ShapeDtypeStruct((chunks, 2, rows, columns), low),
            jax.ShapeDtypeStruct((tokens_here, 3 * width), low),
            jax.ShapeDtypeStruct(small.shape, jnp.float32),
        ),
        in_specs=[pl.BlockSpec(memory_space=pltpu.SMEM)] + [vmem] * len(operands),
        out_specs=(vmem,) * 3,
        scratch_shapes=[
            buf(2, 2, 2, rows, columns),
            buf(2, 2, rows, columns),
            buf(2, rows, columns),
            buf(2, rows, columns),
            buf(rows, columns),
            buf(rows // 2, columns),
            buf(rows // 4, columns),
            buf(2, rows, columns),
            pltpu.VMEM((5,) + small.shape, jnp.float32),
            pltpu.VMEM((5,) + small.shape, jnp.float32),
            dma((8, chunks)),
            dma((8, chunks)),
            dma((5,)),
            dma((5,)),
        ],
        compiler_params=pltpu.CompilerParams(
            collective_id=1, has_side_effects=True, vmem_limit_bytes=63_000_000
        ),
    )(prefix, *operands)


def forward_kernel(prefix_ref, w_query, w_key, w_value, w_out, w_up, w_down, vec_ref, tokens_ref,
                   w_all, vec_full, qkv_ref, context_ref, hidden_ref,
                   vecs, local, send, recv, v_send, v_recv):
    rep, fsdp = lax.axis_index("rep"), lax.axis_index("fsdp")
    rows, width = w_query.shape
    half, quarter, cut = rows // 2, rows // 4, width // 2

    def flip(index, bit):
        return index + bit * (1 - 2 * lax.rem(index // bit, 2))

    near, far = flip(fsdp, 1), flip(fsdp, 2)
    sibling, across = (rep, near), (rep, far)

    def slot(k, owner):
        down = k // 8
        return (1 - down) * (4 * k + owner) + down * (32 + 4 * owner + k - 8)

    barrier = pltpu.get_barrier_semaphore()
    partners = [sibling, across] + [(flip(rep, bit), fsdp) for bit in (1, 2, 4)]
    for partner in partners:
        pl.semaphore_signal(barrier, inc=1, device_id=partner, device_id_type=MESH)
    sources = [w_query, w_key, w_value, w_out]
    sources += [w_up.at[:, j * width : (j + 1) * width] for j in range(4)]
    sources += [w_down.at[j * rows : (j + 1) * rows] for j in range(4)]
    loads = [
        pltpu.make_async_copy(source, w_all.at[slot(k, fsdp)], local.at[k]) for k, source in enumerate(sources)
    ]
    for load in loads:
        load.start()
    pl.semaphore_wait(barrier, len(partners))

    def copies(k, stage, whole=False):
        first = 1 + lax.rem(k, 2)
        second = 3 - first
        (p_one, m_one), (p_two, m_two), (p_three, m_three) = [
            (flip(rep, b), lax.rem(rep // b, 2)) for b in (first, second, 4)
        ]
        columns = pl.ds(pl.multiple_of(m_one * cut, cut), cut)
        two = pl.ds(pl.multiple_of(m_two * half, half), half)
        piece = pl.ds(pl.multiple_of(m_two * half + m_three * quarter, quarter), quarter)
        own, other = w_all.at[slot(k, fsdp)], w_all.at[slot(k, far)]
        if stage == 0:
            ref, to = own if whole else own.at[piece, columns], across
        elif stage == 1:
            ref, to = own, sibling
        elif stage == 2:
            ref, to = other.at[piece, columns], (p_three, fsdp)
        elif stage == 3:
            ref, to = other.at[two, columns], (p_two, fsdp)
        elif stage == 4:
            ref, to = other.at[:, columns], (p_one, fsdp)
        else:
            ref, to = other, sibling
        return pltpu.make_async_remote_copy(
            src_ref=ref, dst_ref=ref, send_sem=send.at[stage, k], recv_sem=recv.at[stage, k],
            device_id=to, device_id_type=MESH)

    def vector(owner, i, to):
        return pltpu.make_async_remote_copy(
            src_ref=vec_ref if i < 2 else vecs.at[owner], dst_ref=vecs.at[owner],
            send_sem=v_send.at[i], recv_sem=v_recv.at[i], device_id=to, device_id_type=MESH)

    v_copies = [vector(fsdp, 0, across), vector(fsdp, 1, sibling), vector(far, 2, sibling)]
    v_copies[0].start()
    v_copies[1].start()
    chunks = len(loads)
    direct = [5, 11]
    for k in range(chunks):
        loads[k].wait()
        copies(k, 0, k in direct).start()
        copies(k, 1).start()
    v_copies[0].wait_recv()
    v_copies[2].start()
    v_copies[1].wait_recv()
    v_copies[2].wait_recv()
    vec_full[...] = as_float(vec_ref[...]) + as_float(vecs[near]) + as_float(vecs[far]) + as_float(vecs[flip(near, 2)])

    pairs = width // PAIR
    length = tokens_ref.shape[0] // prefix_ref.shape[0]
    units = prefix_ref.shape[0] * pairs

    def attend(unit):
        sequence, pair = unit // pairs, lax.rem(unit, pairs)
        here = pl.ds(pl.multiple_of(sequence * length, length), length)
        at = pl.ds(pl.multiple_of(pair * PAIR, PAIR), PAIR)
        query, key, value = qkv_ref[0, here, at], qkv_ref[1, here, at], qkv_ref[2, here, at]
        context_ref[here, at] = attend_pair(query, key, value, prefix_ref[sequence])

    def tick(t, carry):
        for back in range(5):
            k = t - back
            is_direct = lax.rem(k, 6) == 5

            @pl.when((k >= 0) & (k < chunks))
            def _():
                if back < 3:
                    @pl.when(jnp.logical_not(is_direct))
                    def _():
                        copies(k, (0, 2, 3)[back]).wait_recv()
                        copies(k, (2, 3, 4)[back]).start()
                elif back == 3:
                    @pl.when(jnp.logical_not(is_direct))
                    def _():
                        copies(k, 4).wait_recv()

                    @pl.when(is_direct)
                    def _():
                        copies(k, 0, True).wait_recv()

                    copies(k, 5).start()
                else:
                    copies(k, 1).wait_recv()
                    copies(k, 5).wait_recv()

        @pl.when((t >= 4) & (t < 7))
        def _():
            k = t - 4
            weight = w_all[pl.ds(4 * k, 4)].reshape(width, width)
            qkv_ref[k] = (product(tokens_ref[...], weight) + vec_full[pl.ds(k, 1), :]).astype(jnp.bfloat16)

        @pl.when((t >= 7) & (t < 7 + units // 2))
        def _():
            attend(2 * (t - 7))
            attend(2 * (t - 7) + 1)

        return carry

    lax.fori_loop(0, chunks + 4, tick, 0)
    weight = w_all[12:16].reshape(width, width)
    hidden_ref[...] = as_float(tokens_ref[...]) + product(context_ref[...], weight) + vec_full[3:4, :]
    for copy in v_copies:
        copy.wait_send()
    for k in range(chunks):
        copies(k, 0, k in direct).wait_send()
        for stage in (1, 5) if k in direct else (1, 2, 3, 4, 5):
            copies(k, stage).wait_send()


def forward_call(prefix, w_query, w_key, w_value, w_out, w_up, w_down, vectors, tokens):
    rows, width = w_query.shape
    here = tokens.shape[0]
    low = jnp.bfloat16
    dma = pltpu.SemaphoreType.DMA
    vmem = pl.BlockSpec(memory_space=pltpu.VMEM)
    return pl.pallas_call(
        forward_kernel,
        out_shape=(
            jax.ShapeDtypeStruct((48, rows, width), low),
            jax.ShapeDtypeStruct(vectors.shape, jnp.float32),
            jax.ShapeDtypeStruct((3, here, width), low),
            jax.ShapeDtypeStruct((here, width), low),
            jax.ShapeDtypeStruct((here, width), jnp.float32),
        ),
        in_specs=[pl.BlockSpec(memory_space=pltpu.SMEM)]
        + [pl.BlockSpec(memory_space=pl.ANY)] * 6
        + [vmem] * 2,
        out_specs=(vmem,) * 5,
        scratch_shapes=[
            pltpu.VMEM((4,) + vectors.shape, low),
            dma((12,)),
            dma((6, 12)),
            dma((6, 12)),
            dma((3,)),
            dma((3,)),
        ],
        compiler_params=pltpu.CompilerParams(
            collective_id=2, has_side_effects=True, vmem_limit_bytes=48_000_000
        ),
    )(prefix, w_query, w_key, w_value, w_out, w_up, w_down, vectors, tokens)


def body(
    tokens,
    prefix,
    cotangent,
    w_query,
    b_query,
    w_key,
    w_value,
    b_value,
    w_out,
    b_out,
    gain_one,
    shift_one,
    w_up,
    b_up,
    w_down,
    b_down,
    gain_two,
    shift_two,
):
    width = tokens.shape[1]
    vectors = [b_query, b_value, b_out, gain_one, shift_one, b_down, gain_two, shift_two, b_up]
    fsdp = lax.axis_size("fsdp")

    kernels = fsdp == 4 and lax.axis_size("rep") == 8
    if kernels:
        at = lax.axis_index("fsdp") * b_query.shape[0]
        table = jnp.zeros((16, width), jnp.bfloat16)
        stacked = jnp.stack([b_query, jnp.zeros_like(b_query)] + vectors[1:-1])
        table = lax.dynamic_update_slice(table, stacked, (0, at))
        table = lax.dynamic_update_slice(table, b_up[None], (stacked.shape[0] + lax.axis_index("fsdp"), 0))
        w_all, table, qkv, context, hidden = forward_call(
            prefix, w_query, w_key, w_value, w_out, w_up, w_down, table, tokens
        )
        w_up = w_all[16:32].reshape(4, width, width).transpose(1, 0, 2).reshape(width, 4 * width)
        w_down = w_all[32:].reshape(4 * width, width)
        w_out = w_all[12:16].reshape(width, width)
        gain_one, shift_one, b_down, gain_two, shift_two = [table[i] for i in range(4, 9)]
        b_up = table[9:13].reshape(-1)
    else:
        shard = jnp.concatenate([w_query, w_key, w_value, w_out], axis=1)
        heads_w = gather(shard)
        small = gather(jnp.concatenate(vectors)[None])
        pieces = []
        at = 0
        for vector in vectors:
            size = vector.shape[0]
            pieces.append(as_float(small[:, at : at + size].reshape(-1)))
            at += size
        b_query, b_value, b_out, gain_one, shift_one, b_down, gain_two, shift_two, b_up = pieces
        w_up = gather(w_up)
        w_down = gather(w_down)

        w_qkv = heads_w[:, : 3 * width]
        w_out = heads_w[:, 3 * width :]
        qkv = product(tokens, w_qkv)
        query = (qkv[:, :width] + b_query).astype(jnp.bfloat16)
        key = qkv[:, width : 2 * width].astype(jnp.bfloat16)
        value = (qkv[:, 2 * width :] + b_value).astype(jnp.bfloat16)
        context = attention_call(attend_kernel, prefix, (query, key, value), 1)
        hidden = as_float(tokens) + product(context, w_out) + b_out
    normed_one, inverse_one = normalize(hidden)
    inner = (normed_one * gain_one + shift_one).astype(jnp.bfloat16)
    upward = product(inner, w_up) + b_up
    cumulative = 0.5 * (1.0 + lax.erf(upward * 0.7071067811865476))
    active = (upward * cumulative).astype(jnp.bfloat16)
    downward = product(active, w_down) + b_down
    normed_two, inverse_two = normalize(as_float(inner) + downward)
    layer_out = (normed_two * gain_two + shift_two).astype(jnp.bfloat16)

    grad_out = as_float(cotangent)
    grad_gain_two = jnp.sum(grad_out * normed_two, axis=0)
    grad_shift_two = jnp.sum(grad_out, axis=0)
    back_two = norm_back(grad_out * gain_two, normed_two, inverse_two)
    d_down = back_two.astype(jnp.bfloat16)
    grad_b_down = jnp.sum(as_float(d_down), axis=0)
    slope = cumulative + upward * jnp.exp(-0.5 * upward * upward) * 0.3989422804014327
    d_up = (nt(d_down, w_down) * slope).astype(jnp.bfloat16)
    grad_b_up = jnp.sum(as_float(d_up), axis=0)
    d_inner = nt(d_up, w_up) + back_two
    grad_gain_one = jnp.sum(d_inner * normed_one, axis=0)
    grad_shift_one = jnp.sum(d_inner, axis=0)
    back_one = norm_back(d_inner * gain_one, normed_one, inverse_one)
    d_attn = back_one.astype(jnp.bfloat16)
    grad_b_out = jnp.sum(as_float(d_attn), axis=0)
    d_context = nt(d_attn, w_out).astype(jnp.bfloat16)
    sums = [grad_b_out, grad_gain_one, grad_shift_one, grad_b_down, grad_gain_two, grad_shift_two, grad_b_up]
    if kernels:
        none = jnp.zeros((width,), jnp.float32)
        packed = jnp.concatenate([none, none] + sums + [none] * 4).reshape(-1, width)
        chunked, d_qkv, packed = reduce_call(
            prefix, active, d_down, inner, d_up, context, d_attn, tokens, qkv, d_context, packed
        )
        token_grad = back_one
        for part in range(3):
            weight = w_all[4 * part : 4 * part + 4].reshape(width, width)
            token_grad = token_grad + nt(d_qkv[:, part * width : (part + 1) * width], weight)
        rows = chunked.shape[2]
        grad_w_down = chunked[:4].reshape(2, 2, 2, rows, -1).transpose(0, 2, 3, 1, 4).reshape(4 * rows, width)
        wide = chunked[4:].transpose(2, 0, 1, 3).reshape(rows, 8 * width)
        grad_w_up = wide[:, : 4 * width]
        grad_w_out = wide[:, 4 * width : 5 * width]
        grad_qkv = wide[:, 5 * width :]
        packed = packed.reshape(-1)
        mine = lax.axis_index("fsdp")
        vectors, at = [], 0
        for size in [width] * 8 + [4 * width]:
            block = size // fsdp
            vectors.append(lax.dynamic_slice_in_dim(packed, at + mine * block, block))
            at += size
    else:
        grad_w_down = total(tn(active, d_down).astype(jnp.bfloat16))
        grad_w_up = total(tn(inner, d_up).astype(jnp.bfloat16))
        grad_w_out = total(tn(context, d_attn).astype(jnp.bfloat16))
        d_query, d_keys, d_values = attention_call(
            attend_back_kernel, prefix, (query, key, value, d_context), 3
        )
        d_qkv = jnp.concatenate([d_query, d_keys, d_values], axis=1)
        token_grad = back_one + nt(d_qkv, w_qkv)
        grad_qkv = total(tn(tokens, d_qkv).astype(jnp.bfloat16))
        sums = [jnp.sum(as_float(d_query), axis=0), jnp.sum(as_float(d_values), axis=0)] + sums
        packed = jnp.concatenate([s.reshape(fsdp, -1) for s in sums], axis=1)
        small_sum = reduce_group(packed)[0]
        for bit in bits_of("rep"):
            small_sum = small_sum + swap(small_sum, "rep", bit)
        vectors, at = [], 0
        for s in sums:
            size = s.shape[0] // fsdp
            vectors.append(small_sum[at : at + size])
            at += size
    (
        grad_b_query,
        grad_b_value,
        grad_b_out,
        grad_gain_one,
        grad_shift_one,
        grad_b_down,
        grad_gain_two,
        grad_shift_two,
        grad_b_up,
    ) = vectors
    grad_qkv, grad_w_out, grad_w_up, grad_w_down = [
        as_float(g) for g in (grad_qkv, grad_w_out, grad_w_up, grad_w_down)
    ]
    return (
        layer_out,
        token_grad,
        grad_qkv[:, :width],
        grad_b_query,
        grad_qkv[:, width : 2 * width],
        grad_qkv[:, 2 * width :],
        grad_b_value,
        grad_w_out,
        grad_b_out,
        grad_gain_one,
        grad_shift_one,
        grad_w_up,
        grad_b_up,
        grad_w_down,
        grad_b_down,
        grad_gain_two,
        grad_shift_two,
    )


def solution(mesh):
    rows, flat = P(("rep", "fsdp"), None), P(("rep", "fsdp"))
    matrix, vector = P("fsdp", None), P("fsdp")
    placed = (rows, flat, rows) + (
        matrix,
        vector,
        matrix,
        matrix,
        vector,
        matrix,
        vector,
        vector,
        vector,
        matrix,
        vector,
        matrix,
        vector,
        vector,
        vector,
    )
    return jax.shard_map(
        body,
        mesh=mesh,
        in_specs=placed,
        out_specs=(rows, rows) + placed[3:],
        check_vma=False,
    )
```

```python
import functools

import jax
import jax.numpy as jnp
from jax import lax
from jax.experimental import pallas as pl
from jax.experimental.pallas import tpu as pltpu
from jax.sharding import PartitionSpec as P

H = 12
HD = 64
PAIR = 2 * HD

epsilon = 1e-12
masked_fill = -1e30

MESH = pl.DeviceIdType.MESH


def as_float(vector):
    return vector.astype(jnp.float32)


def product(left, right):
    return jnp.dot(left, right, preferred_element_type=jnp.float32)


def nt(left, right):
    return lax.dot_general(left, right, (((1,), (1,)), ((), ())), preferred_element_type=jnp.float32)


def tn(left, right):
    return lax.dot_general(left, right, (((0,), (0,)), ((), ())), preferred_element_type=jnp.float32)


def normalize(hidden):
    centre = hidden - jnp.mean(hidden, axis=-1, keepdims=True)
    inverse = lax.rsqrt(jnp.mean(centre * centre, axis=-1, keepdims=True) + epsilon)
    return (centre * inverse, inverse)


def norm_back(grad_norm, normed, inverse):
    mean_grad = jnp.mean(grad_norm, axis=-1, keepdims=True)
    mean_cross = jnp.mean(grad_norm * normed, axis=-1, keepdims=True)
    return inverse * (grad_norm - mean_grad - normed * mean_cross)


def softmax_parts(query, key, limit):
    length = query.shape[0]
    scores = nt(query, key) * HD ** (-0.5)
    row_pos = lax.broadcasted_iota(jnp.int32, (length, length), 0)
    col_pos = lax.broadcasted_iota(jnp.int32, (length, length), 1)
    visible = (col_pos <= row_pos) | (col_pos < limit)
    scores = jnp.where(visible, scores, masked_fill)
    expo = jnp.exp(scores - jnp.max(scores, axis=-1, keepdims=True))
    return expo * (1.0 / jnp.sum(expo, axis=-1, keepdims=True))


def attend_pair(query, key, value, limit):
    outs = []
    for head in range(2):
        cols = slice(head * HD, (head + 1) * HD)
        prob = softmax_parts(query[:, cols], key[:, cols], limit)
        outs.append(product(prob.astype(jnp.bfloat16), value[:, cols]))
    return jnp.concatenate(outs, axis=1).astype(jnp.bfloat16)


def attend_kernel(prefix_ref, q_ref, k_ref, v_ref, out_ref):
    limit = prefix_ref[pl.program_id(0)]
    out_ref[...] = attend_pair(q_ref[...], k_ref[...], v_ref[...], limit)


def attend_back_pair(query, key, value, d_context, limit):
    d_q, d_k, d_v = [], [], []
    for head in range(2):
        cols = slice(head * HD, (head + 1) * HD)
        q, k, v, d = query[:, cols], key[:, cols], value[:, cols], d_context[:, cols]
        prob = softmax_parts(q, k, limit)
        d_v.append(tn(prob.astype(jnp.bfloat16), d))
        d_prob = as_float(nt(d, v).astype(jnp.bfloat16))
        weighted = prob * d_prob
        d_scores = (weighted - prob * jnp.sum(weighted, axis=-1, keepdims=True)).astype(jnp.bfloat16)
        d_q.append(product(d_scores, k) * HD ** (-0.5))
        d_k.append(tn(d_scores, q) * HD ** (-0.5))
    return [jnp.concatenate(p, axis=1).astype(jnp.bfloat16) for p in (d_q, d_k, d_v)]


def attend_back_kernel(prefix_ref, q_ref, k_ref, v_ref, d_ref, dq_ref, dk_ref, dv_ref):
    limit = prefix_ref[pl.program_id(0)]
    parts = attend_back_pair(q_ref[...], k_ref[...], v_ref[...], d_ref[...], limit)
    for ref, part in zip((dq_ref, dk_ref, dv_ref), parts):
        ref[...] = part


def attention_call(kernel, prefix, operands, outputs):
    rows, width = operands[0].shape
    length = rows // prefix.shape[0]
    block = pl.BlockSpec((length, PAIR), lambda s, h, p: (s, h))
    shape = jax.ShapeDtypeStruct((rows, width), jnp.bfloat16)
    single = outputs == 1
    return pl.pallas_call(
        kernel,
        out_shape=shape if single else [shape] * outputs,
        grid_spec=pltpu.PrefetchScalarGridSpec(
            num_scalar_prefetch=1,
            grid=(prefix.shape[0], width // PAIR),
            in_specs=[block] * len(operands),
            out_specs=block if single else [block] * outputs,
        ),
        cost_estimate=pl.CostEstimate(
            flops=4 * len(operands) * rows * length * width,
            bytes_accessed=2 * rows * width * (len(operands) + outputs),
            transcendentals=rows * length * H,
        ),
    )(prefix, *operands)


def swap(value, axis, bit):
    size = lax.axis_size(axis)
    return lax.ppermute(value, axis, [(i, i ^ bit) for i in range(size)])


def bits_of(axis):
    size = lax.axis_size(axis)
    assert size & (size - 1) == 0
    return [1 << b for b in range(size.bit_length() - 1)]


def gather(block):
    index = lax.axis_index("fsdp")
    rows = block.shape[0]
    rest = block.shape[1:]
    held = block.reshape((1, rows) + rest)
    done = 1
    for bit in reversed(bits_of("fsdp")):
        other = swap(held, "fsdp", bit)
        low = (index & bit) == 0
        held = jnp.stack([jnp.where(low, held, other), jnp.where(low, other, held)], axis=1)
        done *= 2
        held = held.reshape((done, rows) + rest)
    return held.reshape((done * rows,) + rest)


def reduce_group(grad):
    index = lax.axis_index("fsdp")
    count = lax.axis_size("fsdp")
    held = grad.reshape((count, grad.shape[0] // count) + grad.shape[1:])
    for bit in bits_of("fsdp"):
        left = held.shape[0] // 2
        pairs = held.reshape((left, 2) + held.shape[1:])
        low = (index & bit) == 0
        give = jnp.where(low, pairs[:, 1], pairs[:, 0]).astype(jnp.bfloat16)
        keep = jnp.where(low, pairs[:, 0], pairs[:, 1])
        held = as_float(keep) + as_float(swap(give, "fsdp", bit))
        if left > 1:
            held = held.astype(jnp.bfloat16)
    return held[0]


def reduce_replicas(value, order):
    index = lax.axis_index("rep")
    held = value
    for bit in order:
        pairs = held.reshape((2, held.shape[0] // 2) + held.shape[1:])
        low = (index & bit) == 0
        give = jnp.where(low, pairs[1], pairs[0]).astype(jnp.bfloat16)
        keep = jnp.where(low, pairs[0], pairs[1])
        held = as_float(keep) + as_float(swap(give, "rep", bit))
    held = held.astype(jnp.bfloat16)
    for bit in reversed(order):
        other = swap(held, "rep", bit)
        low = (index & bit) == 0
        held = jnp.concatenate([jnp.where(low, held, other), jnp.where(low, other, held)], axis=0)
    return as_float(held)


def total(grad):
    mine = reduce_group(grad)
    bits = bits_of("rep")
    near = bits[:2]
    order_a = bits
    order_b = near[::-1] + bits[2:]
    cut = mine.shape[1] // 2
    return jnp.concatenate(
        [reduce_replicas(mine[:, :cut], order_a), reduce_replicas(mine[:, cut:], order_b)], axis=1
    )


def reduce_kernel(prefix_ref, active_ref, d_down_ref, inner_ref, d_up_ref, context_ref, d_attn_ref, tokens_ref,
                  qkv_ref, d_context_ref, small_ref, out_query, out_key, out_value, out_out, out_up, out_down,
                  d_qkv_ref, small_out, g_ref, core_in, x_in, in_one, in_two, in_three, res, v_held, v_in,
                  send, recv, v_send, v_recv):
    rep, fsdp = lax.axis_index("rep"), lax.axis_index("fsdp")
    core, side = lax.rem(fsdp, 2), fsdp // 2
    chunks = res.shape[0]

    def flip(index, bit):
        return index + bit * (1 - 2 * lax.rem(index // bit, 2))

    sibling = (rep, flip(fsdp, 1))
    across = (rep, flip(fsdp, 2))
    barrier = pltpu.get_barrier_semaphore()
    partners = [sibling, across] + [(flip(rep, bit), fsdp) for bit in (1, 2, 4)]
    for partner in partners:
        pl.semaphore_signal(barrier, inc=1, device_id=partner, device_id_type=MESH)
    pl.semaphore_wait(barrier, len(partners))

    def turns(k):
        first = 1 + lax.rem(k, 2)
        second = 3 - first
        return [(flip(rep, b), lax.rem(rep // b, 2)) for b in (first, second, 4)]

    def copies(k, stage):
        (p_one, m_one), (p_two, m_two), (p_three, m_three) = turns(k)
        rows = x_in.shape[2]
        half, quarter = rows // 2, rows // 4
        mine_two = pl.ds(pl.multiple_of(m_two * half, half), half)
        away_two = pl.ds(pl.multiple_of((1 - m_two) * half, half), half)
        away_three = pl.ds(pl.multiple_of((1 - m_three) * quarter, quarter), quarter)
        piece = pl.ds(pl.multiple_of(m_two * half + m_three * quarter, quarter), quarter)
        if stage == 0:
            src, dst, to = g_ref.at[k, 1 - core], core_in.at[k], sibling
        elif stage == 1:
            src, dst, to = core_in.at[k, 1 - side], x_in.at[k], across
        elif stage == 2:
            src, dst, to = x_in.at[k, 1 - m_one], in_one.at[k], (p_one, fsdp)
        elif stage == 3:
            src, dst, to = in_one.at[k, away_two], in_two.at[k], (p_two, fsdp)
        elif stage == 4:
            src, dst, to = in_two.at[k, away_three], in_three.at[k], (p_three, fsdp)
        elif stage == 5:
            src, dst, to = res.at[k, m_one, piece], res.at[k, m_one, piece], (p_three, fsdp)
        elif stage == 6:
            src, dst, to = res.at[k, m_one, mine_two], res.at[k, m_one, mine_two], (p_two, fsdp)
        else:
            src, dst, to = res.at[k, m_one], res.at[k, m_one], (p_one, fsdp)
        return pltpu.make_async_remote_copy(
            src_ref=src, dst_ref=dst, send_sem=send.at[stage, k], recv_sem=recv.at[stage, k],
            device_id=to, device_id_type=MESH)

    def step(k, stage):
        (_, m_one), (_, m_two), (_, m_three) = turns(k)
        rows = x_in.shape[2]
        half, quarter = rows // 2, rows // 4
        if stage >= 0:
            copies(k, stage).wait_recv()
        if stage == 0:
            core_in[k, 1 - side] = (as_float(g_ref[k, core, 1 - side]) + as_float(core_in[k, 1 - side])).astype(jnp.bfloat16)
        elif stage == 1:
            x_in[k] = (as_float(g_ref[k, core, side]) + as_float(core_in[k, side]) + as_float(x_in[k])).astype(jnp.bfloat16)
        elif stage == 2:
            in_one[k] = (as_float(x_in[k, m_one]) + as_float(in_one[k])).astype(jnp.bfloat16)
        elif stage == 3:
            at = pl.ds(pl.multiple_of(m_two * half, half), half)
            in_two[k] = (as_float(in_one[k, at]) + as_float(in_two[k])).astype(jnp.bfloat16)
        elif stage == 4:
            at = pl.ds(pl.multiple_of(m_three * quarter, quarter), quarter)
            piece = pl.ds(pl.multiple_of(m_two * half + m_three * quarter, quarter), quarter)
            res[k, m_one, piece] = (as_float(in_two[k, at]) + as_float(in_three[k])).astype(jnp.bfloat16)
        elif stage == 7:
            put(k)
        if stage < 7:
            copies(k, stage + 1).start()

    width = tokens_ref.shape[1]

    def v_copy(i):
        to = [sibling, across, (flip(rep, 1), fsdp), (flip(rep, 2), fsdp), (flip(rep, 4), fsdp)][i]
        return pltpu.make_async_remote_copy(
            src_ref=v_held.at[i], dst_ref=v_in.at[i], send_sem=v_send.at[i], recv_sem=v_recv.at[i],
            device_id=to, device_id_type=MESH)

    def v_step(i):
        if i == 0:
            v_held[0] = small_ref[...]
            for row, part in ((0, 0), (1, 2)):
                columns = as_float(d_qkv_ref[:, part * width : (part + 1) * width])
                v_held[0, row : row + 1, :] = jnp.sum(columns, axis=0, keepdims=True)
        else:
            v_copy(i - 1).wait_recv()
            total_now = v_held[i - 1] + v_in[i - 1]
            if i < 5:
                v_held[i] = total_now
            else:
                small_out[...] = total_now
        if i < 5:
            v_copy(i).start()

    def store_columns(k, half, value):
        rows = res.shape[2]
        for x in range(2):
            for c in range(2):
                at = (2 * x + c) * rows
                g_ref[k, c, x, half] = value[at : at + rows].astype(jnp.bfloat16)

    cut = width // 2

    def put(k):
        for half in range(2):
            value = as_float(res[k, half])
            rows = value.shape[0]

            @pl.when(k < 4)
            def _():
                down = pl.ds(pl.multiple_of((k // 2) * cut + half * rows, rows), rows)
                out_down[down, pl.ds(pl.multiple_of(lax.rem(k, 2) * cut, cut), cut)] = value

            @pl.when((k >= 4) & (k < 8))
            def _():
                out_up[:, pl.ds(pl.multiple_of((k - 4) * width + half * cut, cut), cut)] = value

            for last, ref in enumerate((out_out, out_query, out_key, out_value)):
                @pl.when(k == 8 + last)
                def _():
                    ref[:, half * cut : (half + 1) * cut] = value

    def make(k):
        rows = res.shape[2]

        @pl.when(k < 4)
        def _():
            right = d_down_ref[:, pl.ds(pl.multiple_of(lax.rem(k, 2) * cut, cut), cut)]
            for x in range(2):
                for c in range(2):
                    at = (2 * x + c) * width + (k // 2) * cut
                    value = tn(active_ref[:, pl.ds(pl.multiple_of(at, cut), cut)], right)
                    g_ref[k, c, x, 0] = value[:rows].astype(jnp.bfloat16)
                    g_ref[k, c, x, 1] = value[rows:].astype(jnp.bfloat16)

        @pl.when((k >= 4) & (k < 8))
        def _():
            for half in range(2):
                at = pl.multiple_of((k - 4) * width + half * cut, cut)
                store_columns(k, half, tn(inner_ref[...], d_up_ref[:, pl.ds(at, cut)]))

        @pl.when(k == 8)
        def _():
            for half in range(2):
                store_columns(k, half, tn(context_ref[...], d_attn_ref[:, half * cut : (half + 1) * cut]))

        @pl.when(k >= 9)
        def _():
            for half in range(2):
                at = pl.multiple_of((k - 9) * width + half * cut, cut)
                store_columns(k, half, tn(tokens_ref[...], d_qkv_ref[:, pl.ds(at, cut)]))

    pairs = width // PAIR
    length = tokens_ref.shape[0] // prefix_ref.shape[0]
    units = prefix_ref.shape[0] * pairs

    def attend_back(unit):
        sequence, pair = unit // pairs, lax.rem(unit, pairs)
        here = pl.ds(pl.multiple_of(sequence * length, length), length)
        at = pl.multiple_of(pair * PAIR, PAIR)
        limit = prefix_ref[sequence]
        query, key, value = [qkv_ref[part, here, pl.ds(at, PAIR)] for part in range(3)]
        d_context = d_context_ref[here, pl.ds(at, PAIR)]
        parts = attend_back_pair(query, key, value, d_context, limit)
        for part in range(3):
            d_qkv_ref[here, pl.ds(pl.multiple_of(part * width + at, PAIR), PAIR)] = parts[part]

    lead = 3

    def tick(step_at, carry):
        t = step_at - lead
        for stage in range(-1, 8):
            k = step_at - (0 if stage == -1 else 1 if stage == 0 else lead - 1 + stage)

            @pl.when((k >= 0) & (k < chunks))
            def _():
                if stage == -1:
                    make(k)
                step(k, stage)

        @pl.when((t >= 0) & (t < units // 2))
        def _():
            attend_back(2 * step_at - 2 * lead)
            attend_back(2 * step_at - 2 * lead + 1)

        for i in range(6):
            @pl.when(t == units // 2 + i)
            def _():
                v_step(i)
        return carry

    lax.fori_loop(0, chunks + 6 + lead, tick, 0)

    def drain(k, carry):
        for stage in range(8):
            copies(k, stage).wait_send()
        return carry

    lax.fori_loop(0, chunks, drain, 0)
    for i in range(5):
        v_copy(i).wait_send()


def reduce_call(prefix, *operands):
    active, d_down, inner, d_up, context, d_attn, tokens, qkv, d_context, small = operands
    tokens_here, width = tokens.shape
    chunks, rows, columns = 12, width // 4, width // 2
    low = jnp.bfloat16

    def buf(*shape):
        return pltpu.VMEM((chunks,) + shape, low)

    dma = pltpu.SemaphoreType.DMA
    vmem = pl.BlockSpec(memory_space=pltpu.VMEM)
    return pl.pallas_call(
        reduce_kernel,
        out_shape=(
            *[jax.ShapeDtypeStruct((rows, width), jnp.float32)] * 4,
            jax.ShapeDtypeStruct((rows, 4 * width), jnp.float32),
            jax.ShapeDtypeStruct((width, width), jnp.float32),
            jax.ShapeDtypeStruct((tokens_here, 3 * width), low),
            jax.ShapeDtypeStruct(small.shape, jnp.float32),
        ),
        in_specs=[pl.BlockSpec(memory_space=pltpu.SMEM)] + [vmem] * len(operands),
        out_specs=(vmem,) * 8,
        scratch_shapes=[
            buf(2, 2, 2, rows, columns),
            buf(2, 2, rows, columns),
            buf(2, rows, columns),
            buf(rows, columns),
            buf(rows // 2, columns),
            buf(rows // 4, columns),
            buf(2, rows, columns),
            pltpu.VMEM((5,) + small.shape, jnp.float32),
            pltpu.VMEM((5,) + small.shape, jnp.float32),
            dma((8, chunks)),
            dma((8, chunks)),
            dma((5,)),
            dma((5,)),
        ],
        compiler_params=pltpu.CompilerParams(
            collective_id=1, has_side_effects=True, vmem_limit_bytes=63_000_000
        ),
    )(prefix, *operands)


def forward_kernel(prefix_ref, w_query, w_key, w_value, w_out, w_up, w_down, tokens_any, vec_ref,
                   all_query, all_key, all_value, all_out, all_up, all_down,
                   vec_full, qkv_ref, context_ref, hidden_ref,
                   tokens_ref, vecs, local, send, recv, v_send, v_recv):
    rep, fsdp = lax.axis_index("rep"), lax.axis_index("fsdp")
    rows, width = w_query.shape
    square = [all_query, all_key, all_value, all_out]
    half, quarter, cut = rows // 2, rows // 4, width // 2

    def flip(index, bit):
        return index + bit * (1 - 2 * lax.rem(index // bit, 2))

    near, far = flip(fsdp, 1), flip(fsdp, 2)
    sibling, across = (rep, near), (rep, far)

    def place(k, owner, offset=0, count=rows, columns=None):
        base = owner * rows + offset if k < 8 else owner * width + (k - 8) * rows + offset
        here = pl.ds(pl.multiple_of(base, quarter), count)
        first, size = (0, width) if columns is None else (columns, cut)
        if 4 <= k < 8:
            first = first + (k - 4) * width
        ref = square[k] if k < 4 else all_up if k < 8 else all_down
        return ref.at[here, pl.ds(pl.multiple_of(first, cut), size)]

    barrier = pltpu.get_barrier_semaphore()
    partners = [sibling, across] + [(flip(rep, bit), fsdp) for bit in (1, 2, 4)]
    for partner in partners:
        pl.semaphore_signal(barrier, inc=1, device_id=partner, device_id_type=MESH)
    sources = [w_query, w_key, w_value, w_out]
    sources += [w_up.at[:, j * width : (j + 1) * width] for j in range(4)]
    sources += [w_down.at[j * rows : (j + 1) * rows] for j in range(4)]
    loads = [
        pltpu.make_async_copy(source, place(k, fsdp), local.at[k]) for k, source in enumerate(sources)
    ]
    for load in loads:
        load.start()
    tokens_load = pltpu.make_async_copy(tokens_any, tokens_ref, local.at[12])
    tokens_load.start()
    pl.semaphore_wait(barrier, len(partners))

    direct = [10, 11]

    def copies(k, stage):
        first = 1 + k % 2
        second = 3 - first
        (p_one, m_one), (p_two, m_two), (p_three, m_three) = [
            (flip(rep, b), lax.rem(rep // b, 2)) for b in (first, second, 4)
        ]
        columns = m_one * cut
        two = m_two * half
        piece = two + m_three * quarter
        if stage == 0:
            ref = place(k, fsdp) if k in direct else place(k, fsdp, piece, quarter, columns)
            to = across
        elif stage == 1:
            ref, to = place(k, fsdp), sibling
        elif stage == 2:
            ref, to = place(k, far, piece, quarter, columns), (p_three, fsdp)
        elif stage == 3:
            ref, to = place(k, far, two, half, columns), (p_two, fsdp)
        elif stage == 4:
            ref, to = place(k, far, 0, rows, columns), (p_one, fsdp)
        else:
            ref, to = place(k, far), sibling
        return pltpu.make_async_remote_copy(
            src_ref=ref, dst_ref=ref, send_sem=send.at[stage, k], recv_sem=recv.at[stage, k],
            device_id=to, device_id_type=MESH)

    def vector(owner, i, to):
        return pltpu.make_async_remote_copy(
            src_ref=vec_ref if i < 2 else vecs.at[owner], dst_ref=vecs.at[owner],
            send_sem=v_send.at[i], recv_sem=v_recv.at[i], device_id=to, device_id_type=MESH)

    v_copies = [vector(fsdp, 0, across), vector(fsdp, 1, sibling), vector(far, 2, sibling)]
    v_copies[0].start()
    v_copies[1].start()
    chunks = len(loads)
    for k in range(chunks):
        loads[k].wait()
        copies(k, 0).start()
        copies(k, 1).start()
    tokens_load.wait()
    v_copies[0].wait_recv()
    v_copies[2].start()
    v_copies[1].wait_recv()
    v_copies[2].wait_recv()
    vec_full[...] = as_float(vec_ref[...]) + as_float(vecs[near]) + as_float(vecs[far]) + as_float(vecs[flip(near, 2)])

    pairs = width // PAIR
    length = tokens_ref.shape[0] // prefix_ref.shape[0]
    units = prefix_ref.shape[0] * pairs

    def attend(unit):
        sequence, pair = unit // pairs, lax.rem(unit, pairs)
        here = pl.ds(pl.multiple_of(sequence * length, length), length)
        at = pl.ds(pl.multiple_of(pair * PAIR, PAIR), PAIR)
        query, key, value = qkv_ref[0, here, at], qkv_ref[1, here, at], qkv_ref[2, here, at]
        context_ref[here, at] = attend_pair(query, key, value, prefix_ref[sequence])

    def project(k, row):
        value = product(tokens_ref[...], square[k][...])
        if row is not None:
            value = value + vec_full[row : row + 1, :]
        qkv_ref[k] = value.astype(jnp.bfloat16)

    steps = chunks // 2
    for t in range(steps + 4):
        for back in range(5):
            pair = t - back
            if not 0 <= pair < steps:
                continue
            for k in (2 * pair, 2 * pair + 1):
                if back < 3:
                    if k not in direct:
                        copies(k, (0, 2, 3)[back]).wait_recv()
                        copies(k, (2, 3, 4)[back]).start()
                elif back == 3:
                    copies(k, 0 if k in direct else 4).wait_recv()
                    copies(k, 5).start()
                else:
                    copies(k, 1).wait_recv()
                    copies(k, 5).wait_recv()
        if t == 4:
            project(0, 0)
            project(1, None)
        elif t == 5:
            project(2, 1)
        elif t > 5:
            share = units // (steps - 2)
            lax.fori_loop((t - 6) * share, (t - 5) * share, lambda unit, carry: (attend(unit), carry)[1], 0)
    hidden_ref[...] = as_float(tokens_ref[...]) + product(context_ref[...], all_out[...]) + vec_full[2:3, :]
    for copy in v_copies:
        copy.wait_send()
    for k in range(chunks):
        for stage in (0, 1, 5) if k in direct else range(6):
            copies(k, stage).wait_send()


def forward_call(prefix, w_query, w_key, w_value, w_out, w_up, w_down, vectors, tokens):
    rows, width = w_query.shape
    here = tokens.shape[0]
    low = jnp.bfloat16
    dma = pltpu.SemaphoreType.DMA
    vmem = pl.BlockSpec(memory_space=pltpu.VMEM)
    outs = [
        ((width, width), low),
        ((width, width), low),
        ((width, width), low),
        ((width, width), low),
        ((width, 4 * width), low),
        ((4 * width, width), low),
        (vectors.shape, jnp.float32),
        ((3, here, width), low),
        ((here, width), low),
        ((here, width), jnp.float32),
    ]
    return pl.pallas_call(
        forward_kernel,
        out_shape=[jax.ShapeDtypeStruct(*out) for out in outs],
        in_specs=[pl.BlockSpec(memory_space=pltpu.SMEM)]
        + [pl.BlockSpec(memory_space=pltpu.HBM)] * 7
        + [vmem],
        out_specs=[vmem] * len(outs),
        scratch_shapes=[
            pltpu.VMEM((here, width), low),
            pltpu.VMEM((4,) + vectors.shape, low),
            dma((13,)),
            dma((6, 12)),
            dma((6, 12)),
            dma((3,)),
            dma((3,)),
        ],
        compiler_params=pltpu.CompilerParams(
            collective_id=2, has_side_effects=True, vmem_limit_bytes=60_000_000
        ),
    )(prefix, w_query, w_key, w_value, w_out, w_up, w_down, tokens, vectors)


def body(
    tokens,
    prefix,
    cotangent,
    w_query,
    b_query,
    w_key,
    w_value,
    b_value,
    w_out,
    b_out,
    gain_one,
    shift_one,
    w_up,
    b_up,
    w_down,
    b_down,
    gain_two,
    shift_two,
):
    width = tokens.shape[1]
    vectors = [b_query, b_value, b_out, gain_one, shift_one, b_down, gain_two, shift_two, b_up]
    fsdp = lax.axis_size("fsdp")

    kernels = fsdp == 4 and lax.axis_size("rep") == 8
    if kernels:
        at = lax.axis_index("fsdp") * b_query.shape[0]
        stacked = jnp.concatenate(vectors).reshape(-1, b_query.shape[0])
        table = lax.dynamic_update_slice(jnp.zeros((16, width), jnp.bfloat16), stacked, (0, at))
        all_query, all_key, all_value, w_out, w_up, w_down, table, qkv, context, hidden = forward_call(
            prefix, w_query, w_key, w_value, w_out, w_up, w_down, table, tokens
        )
        gain_one, shift_one, b_down, gain_two, shift_two = [table[i] for i in range(3, 8)]
        b_up = table[8:12].reshape(4, fsdp, -1).transpose(1, 0, 2).reshape(-1)
    else:
        shard = jnp.concatenate([w_query, w_key, w_value, w_out], axis=1)
        heads_w = gather(shard)
        small = gather(jnp.concatenate(vectors)[None])
        pieces = []
        at = 0
        for vector in vectors:
            size = vector.shape[0]
            pieces.append(as_float(small[:, at : at + size].reshape(-1)))
            at += size
        b_query, b_value, b_out, gain_one, shift_one, b_down, gain_two, shift_two, b_up = pieces
        w_up = gather(w_up)
        w_down = gather(w_down)

        w_qkv = heads_w[:, : 3 * width]
        w_out = heads_w[:, 3 * width :]
        qkv = product(tokens, w_qkv)
        query = (qkv[:, :width] + b_query).astype(jnp.bfloat16)
        key = qkv[:, width : 2 * width].astype(jnp.bfloat16)
        value = (qkv[:, 2 * width :] + b_value).astype(jnp.bfloat16)
        context = attention_call(attend_kernel, prefix, (query, key, value), 1)
        hidden = as_float(tokens) + product(context, w_out) + b_out
    normed_one, inverse_one = normalize(hidden)
    inner = (normed_one * gain_one + shift_one).astype(jnp.bfloat16)
    upward = product(inner, w_up) + b_up
    cumulative = 0.5 * (1.0 + lax.erf(upward * 0.7071067811865476))
    active = (upward * cumulative).astype(jnp.bfloat16)
    downward = product(active, w_down) + b_down
    normed_two, inverse_two = normalize(as_float(inner) + downward)
    layer_out = (normed_two * gain_two + shift_two).astype(jnp.bfloat16)

    grad_out = as_float(cotangent)
    grad_gain_two = jnp.sum(grad_out * normed_two, axis=0)
    grad_shift_two = jnp.sum(grad_out, axis=0)
    back_two = norm_back(grad_out * gain_two, normed_two, inverse_two)
    d_down = back_two.astype(jnp.bfloat16)
    grad_b_down = jnp.sum(as_float(d_down), axis=0)
    slope = cumulative + upward * jnp.exp(-0.5 * upward * upward) * 0.3989422804014327
    d_up = (nt(d_down, w_down) * slope).astype(jnp.bfloat16)
    grad_b_up = jnp.sum(as_float(d_up), axis=0)
    d_inner = nt(d_up, w_up) + back_two
    grad_gain_one = jnp.sum(d_inner * normed_one, axis=0)
    grad_shift_one = jnp.sum(d_inner, axis=0)
    back_one = norm_back(d_inner * gain_one, normed_one, inverse_one)
    d_attn = back_one.astype(jnp.bfloat16)
    grad_b_out = jnp.sum(as_float(d_attn), axis=0)
    d_context = nt(d_attn, w_out).astype(jnp.bfloat16)
    sums = [grad_b_out, grad_gain_one, grad_shift_one, grad_b_down, grad_gain_two, grad_shift_two, grad_b_up]
    if kernels:
        none = jnp.zeros((width,), jnp.float32)
        packed = jnp.concatenate([none, none] + sums + [none] * 4).reshape(-1, width)
        *weights, d_qkv, packed = reduce_call(
            prefix, active, d_down, inner, d_up, context, d_attn, tokens, qkv, d_context, packed
        )
        token_grad = back_one
        for part, weight in enumerate((all_query, all_key, all_value)):
            token_grad = token_grad + nt(d_qkv[:, part * width : (part + 1) * width], weight)
        packed = packed.reshape(-1)
        mine = lax.axis_index("fsdp")
        vectors, at = [], 0
        for size in [width] * 8 + [4 * width]:
            block = size // fsdp
            vectors.append(lax.dynamic_slice_in_dim(packed, at + mine * block, block))
            at += size
    else:
        grad_w_down = total(tn(active, d_down).astype(jnp.bfloat16))
        grad_w_up = total(tn(inner, d_up).astype(jnp.bfloat16))
        grad_w_out = total(tn(context, d_attn).astype(jnp.bfloat16))
        d_query, d_keys, d_values = attention_call(
            attend_back_kernel, prefix, (query, key, value, d_context), 3
        )
        d_qkv = jnp.concatenate([d_query, d_keys, d_values], axis=1)
        token_grad = back_one + nt(d_qkv, w_qkv)
        grad_qkv = total(tn(tokens, d_qkv).astype(jnp.bfloat16))
        sums = [jnp.sum(as_float(d_query), axis=0), jnp.sum(as_float(d_values), axis=0)] + sums
        packed = jnp.concatenate([s.reshape(fsdp, -1) for s in sums], axis=1)
        weights = [grad_qkv[:, part * width : (part + 1) * width] for part in range(3)]
        weights = [as_float(g) for g in (*weights, grad_w_out, grad_w_up, grad_w_down)]
        small_sum = reduce_group(packed)[0]
        for bit in bits_of("rep"):
            small_sum = small_sum + swap(small_sum, "rep", bit)
        vectors, at = [], 0
        for s in sums:
            size = s.shape[0] // fsdp
            vectors.append(small_sum[at : at + size])
            at += size
    (
        grad_b_query,
        grad_b_value,
        grad_b_out,
        grad_gain_one,
        grad_shift_one,
        grad_b_down,
        grad_gain_two,
        grad_shift_two,
        grad_b_up,
    ) = vectors
    grad_w_query, grad_w_key, grad_w_value, grad_w_out, grad_w_up, grad_w_down = weights
    return (
        layer_out,
        token_grad,
        grad_w_query,
        grad_b_query,
        grad_w_key,
        grad_w_value,
        grad_b_value,
        grad_w_out,
        grad_b_out,
        grad_gain_one,
        grad_shift_one,
        grad_w_up,
        grad_b_up,
        grad_w_down,
        grad_b_down,
        grad_gain_two,
        grad_shift_two,
    )


def solution(mesh):
    rows, flat = P(("rep", "fsdp"), None), P(("rep", "fsdp"))
    matrix, vector = P("fsdp", None), P("fsdp")
    placed = (rows, flat, rows) + (
        matrix,
        vector,
        matrix,
        matrix,
        vector,
        matrix,
        vector,
        vector,
        vector,
        matrix,
        vector,
        matrix,
        vector,
        vector,
        vector,
    )
    return jax.shard_map(
        body,
        mesh=mesh,
        in_specs=placed,
        out_specs=(rows, rows) + placed[3:],
        check_vma=False,
    )
```
